32 devices in a mesh: virt: 8 (over z, x), pair: 4 (over y, core).
Axes of the slice: x: 2, y: 2, z: 4, core: 2. Of those that a mesh axis runs over, the one named last changes fastest.
Arguments:
- amplitudes: bfloat16 [8, 1024, 2, 1024], P('pair'), may hold values from -6 to 6
- integrals: bfloat16 [2, 512, 8, 65536], P(None, None, None, ('virt', 'pair')), may hold values from -0.125 to 0.125
- virt_counts: int32 [8], replicated, may hold values from 32 to 64, as said below
- pair_counts: int32 [8], replicated, may hold values from 512 to 1024, as said below
- pair_list: int32 [8, 1024, 2], P('pair'), may hold values from 0 to 99
- eps_occ: float32 [100], replicated, may hold values from -2 to -0.3
- eps_virt: float32 [512], replicated, may hold values from 0.3 to 4
Outputs:
- update: bfloat16 [8, 1024, 32768], P('pair', None, 'virt')
- pair_energy: float32 [8, 1024], P('pair', 'virt')
The draws below stay inside these ranges and needn't reach their ends.
Inputs may be any that keep to these rules, and one draw needn't show every extreme that they name: virt_counts[0] = 64; every count is at least 32. `pair_counts`: some pair symmetry has exactly 1024 pairs; every count is at least 512.
All inputs are finite; a program needn't handle non-finite values.
Results may differ from the reference program's by a relative error of at most 0.001.
Values may be sent and summed in bfloat16 or wider, within the bound.
A program may use at most 192 MiB of HBM per device.

```python
import math
import jax
import jax.numpy as jnp
from jax import lax

IRREPS = 8
NV = 512
NOCC = 100
BLK = 64
CS = 16
SLABS = 2
KS = 1024
PCAP = 1024


def draw_virt_counts(key, part):
    counts = jax.random.randint(key, (IRREPS,), BLK // 2, BLK + 1)
    return counts.at[0].set(BLK).astype(jnp.int32)


def draw_pair_counts(key, part):
    first, second = jax.random.split(jax.random.fold_in(key, 11))
    counts = jax.random.randint(first, (IRREPS,), PCAP // 2, PCAP + 1)
    where_full = jax.random.randint(second, (), 0, IRREPS)
    return counts.at[where_full].set(PCAP).astype(jnp.int32)


def set_ends(entries, stream_key, smallest, largest):
    dims = entries.shape
    index_at = [jax.random.randint(jax.random.fold_in(stream_key, axis), (), 0, dims[axis]) for axis in range(len(dims))]
    entries = entries.at[tuple(index_at)].set(smallest)
    longest = dims.index(max(dims))
    index_at[longest] = (index_at[longest] + 1) % dims[longest]
    return entries.at[tuple(index_at)].set(largest)


def levels(stream_key, dims, cuts, least, largest):
    factor_of = 1.0
    for position, shards_of in cuts:
        heights = jax.random.uniform(jax.random.fold_in(jax.random.fold_in(stream_key, 6), position), (shards_of,), jnp.float32, least / len(cuts), largest / len(cuts))
        factor_of = factor_of * jnp.repeat(jnp.exp(heights), dims[position] // shards_of).reshape((-1,) + (1,) * (len(dims) - 1 - position))
    return factor_of


def centred(rng, extent, deviation, limit, pieces=(), held_as=jnp.bfloat16):
    result = jax.random.normal(rng, extent, jnp.float32) * deviation
    if len(pieces) > 0:
        result = levels(rng, extent, pieces, -0.22, 0.18) * result
    return jnp.clip(result, min=-limit, max=limit).astype(held_as)


def setup_inputs(seed: int = 0) -> dict:
    seeds = jax.random.split(jax.random.key(seed), 8)
    return {
        "amplitudes": centred(seeds[0], (IRREPS, PCAP, SLABS, KS), 1.0, 6.0, ((0, 4),)),
        "integrals": centred(seeds[1], (SLABS, NV, IRREPS, BLK * KS), (KS * SLABS) ** -0.5, 0.125, ((3, 32),)),
        "virt_counts": draw_virt_counts(jax.random.fold_in(seeds[7], 71), 0),
        "pair_counts": draw_pair_counts(jax.random.fold_in(seeds[7], 71), 0),
        "pair_list": set_ends(jax.random.randint(seeds[4], (IRREPS, PCAP, 2), 0, NOCC), jax.random.fold_in(seeds[4], 1), 0, NOCC - 1).astype(jnp.int32),
        "eps_occ": jnp.clip(jax.random.uniform(seeds[5], (NOCC,), jnp.float32, -2.0, -0.3), -2.0, -0.3),
        "eps_virt": jnp.clip(jnp.exp(jax.random.uniform(seeds[6], (NV,), jnp.float32, math.log(0.3), math.log(4.0))), 0.3, 4.0),
    }


def reference(amplitudes, integrals, virt_counts, pair_counts, pair_list, eps_occ, eps_virt):
    slots = jnp.arange(BLK, dtype=jnp.int32)
    live_virt = slots[None, :] < virt_counts[:, None]
    a_index = jnp.arange(NV, dtype=jnp.int32)
    a_irrep = a_index // BLK
    a_slot = a_index % BLK
    live_a = jnp.take(live_virt.reshape(-1), a_irrep * BLK + a_slot)
    eps_table = eps_virt.reshape(IRREPS, BLK)
    row_index = jnp.arange(PCAP, dtype=jnp.int32)

    def one_irrep(h):
        dmask = jnp.tile(live_virt[h], CS).astype(jnp.bfloat16)
        masked = amplitudes[h] * dmask[None, None, :]
        ladder = jnp.zeros((PCAP, NV * BLK), jnp.float32)
        for s in range(SLABS):
            block = integrals[s][:, h, :].reshape(NV * BLK, KS)
            ladder = ladder + lax.dot_general(masked[:, s, :], block, (((1,), (1,)), ((), ())), preferred_element_type=jnp.float32)
        ladder = ladder.reshape(PCAP, NV, BLK)
        b_irrep = jnp.bitwise_xor(a_irrep, h)
        eps_b = eps_table[b_irrep]
        live_b = live_virt[b_irrep]
        pairs = pair_list[h]
        occ = eps_occ[pairs[:, 0]] + eps_occ[pairs[:, 1]]
        denom = (eps_virt[:, None] + eps_b)[None, :, :] - occ[:, None, None]
        live = (row_index < pair_counts[h])[:, None, None] & live_a[None, :, None] & live_b[None, :, :]
        ratio = jnp.where(live, ladder / denom, jnp.zeros_like(ladder))
        update = ratio.astype(jnp.bfloat16).reshape(PCAP, NV * BLK)
        energy = jnp.sum(ratio * ladder, axis=(1, 2)) / (NV * BLK)
        return update, energy

    updates, energies = lax.map(one_irrep, jnp.arange(IRREPS, dtype=jnp.int32))
    return updates, energies
```

```python
import functools

import jax
import jax.numpy as jnp
from jax import lax
from jax.experimental import pallas as pl
from jax.experimental.pallas import tpu as pltpu
from jax.sharding import PartitionSpec as P

IRREPS = 8
NV = 512
BLK = 64
CS = 16
SLABS = 2
A_UNIT = 16
MESH = pl.DeviceIdType.MESH


def pick_counts(irrep_ids, table):
    onehot = irrep_ids[..., None] == jnp.arange(table.shape[0], dtype=jnp.int32)
    return jnp.sum(jnp.where(onehot, table, 0), axis=-1)


def shards(amplitudes, integrals, virt_counts, pair_counts, pair_list, eps_occ, eps_virt):
    local_irreps = amplitudes.shape[0]
    rows = amplitudes.shape[1]
    width = amplitudes.shape[3]
    n_virt = lax.axis_size("virt")
    n_pair = lax.axis_size("pair")
    a_local = NV // n_virt
    irrep_ids = lax.axis_index("pair") * local_irreps + jnp.arange(local_irreps, dtype=jnp.int32)
    slots = jnp.arange(BLK, dtype=jnp.int32)
    live_d = slots[None, :] < pick_counts(irrep_ids, virt_counts)[:, None]
    dmask = jnp.tile(live_d, (1, CS)).astype(jnp.bfloat16)
    masked = amplitudes * dmask[:, None, None, :]
    ladder = jnp.zeros((local_irreps, rows, a_local, BLK), jnp.float32)
    for s in range(SLABS):
        piece = integrals[s]
        moved = lax.all_to_all(
            lax.all_to_all(piece, "virt", split_axis=0, concat_axis=2, tiled=True),
            "pair",
            split_axis=1,
            concat_axis=2,
            tiled=True,
        )
        moved = moved.reshape(a_local, local_irreps, n_pair, n_virt, -1)
        moved = jnp.transpose(moved, (0, 1, 3, 2, 4)).reshape(a_local, local_irreps, BLK, width)
        ladder = ladder + jnp.einsum(
            "hrk,ahsk->hras", masked[:, :, s, :], moved, preferred_element_type=jnp.float32
        )
    a_global = lax.axis_index("virt") * a_local + jnp.arange(a_local, dtype=jnp.int32)
    a_irrep = a_global // BLK
    a_slot = a_global % BLK
    live_a = a_slot < pick_counts(a_irrep, virt_counts)
    eps_a = lax.dynamic_slice_in_dim(eps_virt, lax.axis_index("virt") * a_local, a_local)
    b_irrep = jnp.bitwise_xor(a_irrep[None, :], irrep_ids[:, None])
    b_onehot = (b_irrep[..., None] == jnp.arange(IRREPS, dtype=jnp.int32)).astype(jnp.float32)
    eps_table = eps_virt.reshape(IRREPS, BLK)
    eps_b = jnp.einsum("hag,gs->has", b_onehot, eps_table, precision=lax.Precision.HIGHEST)
    live_b = slots[None, None, :] < pick_counts(b_irrep, virt_counts)[..., None]
    occ_onehot = pair_list[..., None] == jnp.arange(eps_occ.shape[0], dtype=jnp.int32)
    occ_terms = jnp.sum(jnp.where(occ_onehot, eps_occ, 0.0), axis=-1)
    occ = occ_terms[:, :, 0] + occ_terms[:, :, 1]
    live_rows = (
        jnp.arange(rows, dtype=jnp.int32)[None, :] < pick_counts(irrep_ids, pair_counts)[:, None]
    )
    denom = (eps_a[None, :, None] + eps_b)[:, None, :, :] - occ[:, :, None, None]
    live = live_rows[:, :, None, None] & live_a[None, None, :, None] & live_b[:, None, :, :]
    ratio = jnp.where(live, ladder / denom, jnp.zeros_like(ladder))
    update = ratio.astype(jnp.bfloat16).reshape(local_irreps, rows, a_local * BLK)
    partial_value = jnp.sum(ratio * ladder, axis=(2, 3)) / (NV * BLK)
    energy = lax.psum_scatter(partial_value, "virt", scatter_dimension=1, tiled=True)
    return (update, energy)


def flip_bits(index, pattern, count):
    flipped = 0
    weight = 1
    while weight < count:
        bit = (index // weight) % 2
        mine = (pattern // weight) % 2
        flipped = flipped + weight * (bit + mine - 2 * bit * mine)
        weight *= 2
    return flipped


def step_plan(count, units):
    plan = []
    for i in range(count):
        sizes = [2] * (units // 2) + [1] * (units % 2)
        if i == 0:
            sizes = [1, 1] + sizes[1:]
        if i == count - 1 and sizes[-1] == 2:
            sizes = sizes[:-1] + [1, 1]
        start = 0
        for size in sizes:
            plan.append((count - 1 - i, start, size))
            start += size
    return plan


def unit_matrix(count, outer, inner):
    rows = lax.broadcasted_iota(jnp.int32, (count * outer * inner, count * outer * inner), 0)
    cols = lax.broadcasted_iota(jnp.int32, (count * outer * inner, count * outer * inner), 1)
    unit = rows // (outer * inner)
    within = rows % (outer * inner)
    source = unit * (outer * inner) + (within % inner) * outer + within // inner
    return (source == cols).astype(jnp.float32).astype(jnp.bfloat16)


def ladder_kernel(
    n_virt, n_pair, irreps_here, depth, parts_sb, energy_scale,
    eri_ref, amps_ref, pair_ref, row_ref, vcount_ref, pcount_ref, eocc_ref, evirt_ref,
    got_ref, recv_ref, energy_ref,
    x_buf, stage, y_buf, out_buf, a_buf, amps, sort_in, sort_out, pick, levels, occ, cols_buf, terms, parts,
    x_sem, y_sem, own_sem, keep_sem, send_sem, recv_sem, out_sem, got_sem, term_sem, part_sem, a_sem,
):
    me_v = lax.axis_index("virt")
    me_p = lax.axis_index("pair")
    slabs = eri_ref.shape[0]
    loc = eri_ref.shape[2]
    irreps = irreps_here * n_pair
    ks = amps.shape[2]
    nrows = amps.shape[3]
    nv = row_ref.shape[1]
    nocc = eocc_ref.shape[0]
    a_local = nv // n_virt
    unit_rows = A_UNIT * irreps
    sb_here = n_pair * parts_sb
    out_rows = A_UNIT * sb_here
    plan = step_plan(n_virt, a_local // A_UNIT)
    steps = len(plan)
    e_cols = nrows // n_virt
    tile_n = 512
    tile_r = 256
    a_rows = a_buf.shape[1]
    peers = [d for d in range(2, n_pair)] + [1]
    first_unit = []
    total = 0
    for _, _, size in plan:
        first_unit.append(total)
        total += size

    def target(t):
        return flip_bits(me_v, plan[t][0], n_virt)

    def x_copy(t):
        _, start, size = plan[t]
        at = pl.multiple_of((target(t) * (a_local // A_UNIT) + start) * unit_rows, unit_rows)
        return pltpu.make_async_copy(
            eri_ref.at[:, pl.ds(at, size * unit_rows), :], x_buf.at[:, 0 : size * unit_rows, :], x_sem
        )

    def a_copy(block):
        per = nrows // a_rows
        at = pl.multiple_of((block % per) * a_rows, a_rows)
        return pltpu.make_async_copy(
            amps_ref.at[block // per, pl.ds(at, a_rows)], a_buf.at[block % 2], a_sem.at[block % 2]
        )

    def pair_copy(t, d):
        peer = flip_bits(me_p, d, n_pair)
        size = plan[t][2]
        return pltpu.make_async_remote_copy(
            src_ref=stage.at[t % depth, 0:size, peer],
            dst_ref=recv_ref.at[first_unit[t] : first_unit[t] + size, me_p],
            send_sem=send_sem.at[t % depth, d - 1],
            recv_sem=recv_sem.at[t, d - 1],
            device_id=(me_v, peer),
            device_id_type=MESH,
        )

    def own_copy(t):
        size = plan[t][2]
        return pltpu.make_async_copy(
            stage.at[t % depth, 0:size, me_p],
            recv_ref.at[first_unit[t] : first_unit[t] + size, me_p],
            own_sem.at[t % depth],
        )

    def out_copy(t, hh):
        d, start, size = plan[t]
        here = out_buf.at[first_unit[t] : first_unit[t] + size, hh]
        there = got_ref.at[hh, start : start + size, :, me_v]
        if d == 0:
            return pltpu.make_async_copy(here, there, keep_sem.at[t - (steps - keep_sem.shape[0]), hh])
        return pltpu.make_async_remote_copy(
            src_ref=here,
            dst_ref=there,
            send_sem=out_sem.at[t, hh],
            recv_sem=got_sem.at[t, hh],
            device_id=(target(t), me_p),
            device_id_type=MESH,
        )

    def part_copy(d):
        dest = flip_bits(me_v, d, n_virt)
        cols = pl.ds(pl.multiple_of(dest * e_cols, e_cols), e_cols)
        return pltpu.make_async_remote_copy(
            src_ref=terms.at[:, cols],
            dst_ref=parts.at[d - 1],
            send_sem=term_sem.at[d - 1],
            recv_sem=part_sem.at[d - 1],
            device_id=(dest, me_p),
            device_id_type=MESH,
        )

    def prepare(t):
        size = plan[t][2]
        n = size * unit_rows
        x_copy(t).wait()

        def sort_tile(i, carry):
            cols = pl.ds(pl.multiple_of(i * tile_n, tile_n), tile_n)
            for s in range(slabs):
                sorted_rows = jnp.dot(
                    sort_in[0:n, 0:n], x_buf[s, 0:n, cols], preferred_element_type=jnp.float32
                ).astype(jnp.bfloat16)
                for u in range(size):
                    for h in range(irreps):
                        at = u * unit_rows + h * A_UNIT
                        stage[
                            t % depth, u, h // irreps_here, h % irreps_here, s, :, cols
                        ] = sorted_rows[at : at + A_UNIT]
            return carry

        lax.fori_loop(0, loc // tile_n, sort_tile, 0)
        if t + 1 < steps:
            x_copy(t + 1).start()
        for d in peers:
            pair_copy(t, d).start()
        own_copy(t).start()

    def load_amps(hh):
        per = nrows // a_rows
        h = me_p * irreps_here + hh
        slot = lax.broadcasted_iota(jnp.int32, (1, tile_r), 1) % BLK
        dmask = jnp.where(slot < vcount_ref[h], 1.0, 0.0).astype(jnp.bfloat16)

        def block(i, carry):
            now = hh * per + i
            a_copy(now).wait()

            @pl.when(now + 1 < irreps_here * per)
            def _():
                a_copy(now + 1).start()

            rows = pl.ds(pl.multiple_of(i * a_rows, a_rows), a_rows)
            for c in range(ks // tile_r):
                lanes = slice(c * tile_r, (c + 1) * tile_r)
                mixed = a_buf[now % 2, :, :, lanes].reshape(a_rows * slabs, tile_r)
                split = jnp.dot(pick[0], mixed, preferred_element_type=jnp.float32).astype(jnp.bfloat16) * dmask
                turned = lax.dot_general(
                    pick[1], split, (((1,), (1,)), ((), ())), preferred_element_type=jnp.float32
                ).astype(jnp.bfloat16)
                for s in range(slabs):
                    amps[hh, s, lanes, rows] = turned[:, s * a_rows : (s + 1) * a_rows]
            return carry

        lax.fori_loop(0, per, block, 0)

    def fetch(t):
        size = plan[t][2]
        for d in range(1, n_pair):
            pair_copy(t, d).wait_recv()
        own_copy(t).wait()
        load = pltpu.make_async_copy(
            recv_ref.at[first_unit[t] : first_unit[t] + size], y_buf.at[0:size], y_sem
        )
        load.start()
        load.wait()

    def compute(t, hh):
        _, start, size = plan[t]
        n = size * out_rows
        h = me_p * irreps_here + hh
        bases = []
        lives = []
        for u in range(size):
            a_first = target(t) * a_local + (start + u) * A_UNIT
            a_irrep = a_first // BLK
            b_irrep = flip_bits(a_irrep, h, irreps)
            eps_a = levels[pl.ds(pl.multiple_of(a_first, A_UNIT), A_UNIT), 0:1]
            a_slot = a_first % BLK + lax.broadcasted_iota(jnp.int32, (A_UNIT, 1), 0)
            live_a = jnp.where(a_slot < vcount_ref[a_irrep], 1.0, 0.0)
            for b in range(sb_here):
                b_slot = me_v * sb_here + b
                bases.append(eps_a + evirt_ref[b_irrep * BLK + b_slot])
                lives.append(live_a * jnp.where(b_slot < vcount_ref[b_irrep], 1.0, 0.0))
        cols_buf[0, 0:n, :] = jnp.concatenate(bases, axis=0)
        cols_buf[1, 0:n, :] = jnp.concatenate(lives, axis=0)

        def tile(i, carry):
            cols = pl.ds(pl.multiple_of(i * tile_r, tile_r), tile_r)
            ladder = None
            for s in range(slabs):
                left = jnp.concatenate(
                    [
                        y_buf[u, p, hh, s, :, j * ks : (j + 1) * ks]
                        for u in range(size)
                        for p in range(n_pair)
                        for j in range(parts_sb)
                    ],
                    axis=0,
                )
                term = jnp.dot(left, amps[hh, s, :, cols], preferred_element_type=jnp.float32)
                ladder = term if ladder is None else ladder + term
            denom = cols_buf[0, 0:n, :] - occ[hh : hh + 1, cols]
            live = cols_buf[1, 0:n, :] * occ[irreps_here + hh : irreps_here + hh + 1, cols]
            ratio = jnp.where(live > 0.5, ladder / denom, 0.0)
            terms[hh : hh + 1, cols] += jnp.sum(ratio * ladder, axis=0, keepdims=True)
            update = jnp.dot(
                sort_out[0:n, 0:n], ratio.astype(jnp.bfloat16), preferred_element_type=jnp.float32
            ).astype(jnp.bfloat16)
            out_buf[first_unit[t] : first_unit[t] + size, hh, :, :, cols] = update.reshape(
                size, A_UNIT, sb_here, tile_r
            )
            return carry

        lax.fori_loop(0, nrows // tile_r, tile, 0)
        out_copy(t, hh).start()

    def tables():
        sort_out[...] = unit_matrix(2, A_UNIT, sb_here)
        for i in range(nv // 128):
            piece = jnp.broadcast_to(row_ref[0:1, i * 128 : (i + 1) * 128], (128, 128))
            levels[i * 128 : (i + 1) * 128, :] = piece.T
        index = pair_ref[...]

        def add_level(o, acc):
            return acc + jnp.where(index == o, eocc_ref[o], 0.0)

        picked = lax.fori_loop(0, nocc, add_level, jnp.zeros(index.shape, jnp.float32))
        slot = lax.broadcasted_iota(jnp.int32, (1, nrows), 1)
        for hh in range(irreps_here):
            occ[hh : hh + 1, :] = picked[hh, 0:1, :] + picked[hh, 1:2, :]
            live = slot < pcount_ref[me_p * irreps_here + hh]
            occ[irreps_here + hh : irreps_here + hh + 1, :] = jnp.where(live, 1.0, 0.0)
        pick[0] = unit_matrix(1, slabs, a_rows)
        pick[1] = unit_matrix(1, 1, tile_r)
        terms[...] = jnp.zeros_like(terms)

    x_copy(0).start()
    a_copy(0).start()
    barrier = pltpu.get_barrier_semaphore()
    for d in range(1, n_pair):
        pl.semaphore_signal(barrier, inc=1, device_id=(me_v, flip_bits(me_p, d, n_pair)), device_id_type=MESH)
    for d in range(1, n_virt):
        pl.semaphore_signal(barrier, inc=1, device_id=(flip_bits(me_v, d, n_virt), me_p), device_id_type=MESH)
    sort_in[...] = unit_matrix(2, irreps, A_UNIT)
    pl.semaphore_wait(barrier, n_pair - 1 + n_virt - 1)

    ahead = 0
    while ahead < 2:
        prepare(ahead)
        ahead += 1
    tables()
    for hh in range(irreps_here):
        load_amps(hh)
        if hh == 0:
            fetch(0)
        compute(0, hh)
        if ahead < depth:
            prepare(ahead)
            ahead += 1
    while ahead < depth:
        prepare(ahead)
        ahead += 1
    for t in range(steps):
        if t > 0:
            fetch(t)
            for hh in range(irreps_here):
                compute(t, hh)
        for d in range(1, n_pair):
            pair_copy(t, d).wait_send()
        if t + depth < steps:
            prepare(t + depth)
    for d in range(1, n_virt):
        part_copy(d).start()
    for d in range(1, n_virt):
        part_copy(d).wait()
    mine = terms[:, pl.ds(pl.multiple_of(me_v * e_cols, e_cols), e_cols)]
    for d in range(1, n_virt):
        mine = mine + parts[d - 1]
    energy_ref[...] = mine / energy_scale
    for t in range(steps):
        for hh in range(irreps_here):
            out_copy(t, hh).wait()


def turn_kernel(in_ref, out_ref):
    size = 256
    eye = unit_matrix(1, 1, size)
    for i in range(in_ref.shape[1] // size):
        for j in range(in_ref.shape[2] // size):
            block = in_ref[0, i * size : (i + 1) * size, j * size : (j + 1) * size]
            out_ref[0, j * size : (j + 1) * size, i * size : (i + 1) * size] = lax.dot_general(
                eye, block, (((1,), (1,)), ((), ())), preferred_element_type=jnp.float32
            ).astype(jnp.bfloat16)


def fused_shards(amplitudes, integrals, virt_counts, pair_counts, pair_list, eps_occ, eps_virt):
    irreps_here, rows, slabs, ks = amplitudes.shape
    n_virt = lax.axis_size("virt")
    n_pair = lax.axis_size("pair")
    nv = integrals.shape[1]
    irreps = integrals.shape[2]
    loc = integrals.shape[3]
    depth = 4
    a_local = nv // n_virt
    units = a_local // A_UNIT
    plan = step_plan(n_virt, units)
    steps = len(plan)
    kept = sum(1 for d, _, _ in plan if d == 0)
    parts_sb = loc // ks
    sb_here = n_pair * parts_sb
    a_rows = 256 // slabs

    eri = integrals.reshape(slabs, nv * irreps, loc)
    pairs = jnp.transpose(pair_list, (0, 2, 1))
    vmem = pl.BlockSpec(memory_space=pltpu.VMEM)
    smem = pl.BlockSpec(memory_space=pltpu.SMEM)
    hbm = pl.BlockSpec(memory_space=pl.ANY)
    got, _, energy = pl.pallas_call(
        functools.partial(ladder_kernel, n_virt, n_pair, irreps_here, depth, parts_sb, nv * BLK),
        out_shape=(
            jax.ShapeDtypeStruct((irreps_here, units, A_UNIT, n_virt, sb_here, rows), jnp.bfloat16),
            jax.ShapeDtypeStruct((units * n_virt, n_pair, irreps_here, slabs, A_UNIT, loc), jnp.bfloat16),
            jax.ShapeDtypeStruct((irreps_here, rows // n_virt), jnp.float32),
        ),
        in_specs=[hbm, hbm, vmem, vmem, smem, smem, smem, smem],
        out_specs=(hbm, hbm, vmem),
        scratch_shapes=[
            pltpu.VMEM((slabs, 2 * A_UNIT * irreps, loc), jnp.bfloat16),
            pltpu.VMEM((depth, 2, n_pair, irreps_here, slabs, A_UNIT, loc), jnp.bfloat16),
            pltpu.VMEM((2, n_pair, irreps_here, slabs, A_UNIT, loc), jnp.bfloat16),
            pltpu.VMEM((units * n_virt, irreps_here, A_UNIT, sb_here, rows), jnp.bfloat16),
            pltpu.VMEM((2, a_rows, slabs, ks), jnp.bfloat16),
            pltpu.VMEM((irreps_here, slabs, ks, rows), jnp.bfloat16),
            pltpu.VMEM((2 * A_UNIT * irreps, 2 * A_UNIT * irreps), jnp.bfloat16),
            pltpu.VMEM((2 * A_UNIT * sb_here, 2 * A_UNIT * sb_here), jnp.bfloat16),
            pltpu.VMEM((2, 256, 256), jnp.bfloat16),
            pltpu.VMEM((nv, 128), jnp.float32),
            pltpu.VMEM((2 * irreps_here, rows), jnp.float32),
            pltpu.VMEM((2, 2 * A_UNIT * sb_here, 1), jnp.float32),
            pltpu.VMEM((irreps_here, rows), jnp.float32),
            pltpu.VMEM((n_virt - 1, irreps_here, rows // n_virt), jnp.float32),
            pltpu.SemaphoreType.DMA,
            pltpu.SemaphoreType.DMA,
            pltpu.SemaphoreType.DMA((depth,)),
            pltpu.SemaphoreType.DMA((kept, irreps_here)),
            pltpu.SemaphoreType.DMA((depth, n_pair - 1)),
            pltpu.SemaphoreType.DMA((steps, n_pair - 1)),
            pltpu.SemaphoreType.DMA((steps, irreps_here)),
            pltpu.SemaphoreType.DMA((steps, irreps_here)),
            pltpu.SemaphoreType.DMA((n_virt - 1,)),
            pltpu.SemaphoreType.DMA((n_virt - 1,)),
            pltpu.SemaphoreType.DMA((2,)),
        ],
        compiler_params=pltpu.CompilerParams(
            collective_id=0, has_side_effects=True, vmem_limit_bytes=60 * 1024 * 1024
        ),
    )(eri, amplitudes, pairs, eps_virt.reshape(1, nv), virt_counts, pair_counts, eps_occ, eps_virt)
    flat = got.reshape(irreps_here, a_local * BLK, rows)
    update = pl.pallas_call(
        turn_kernel,
        grid=(irreps_here,),
        out_shape=jax.ShapeDtypeStruct((irreps_here, rows, a_local * BLK), jnp.bfloat16),
        in_specs=[pl.BlockSpec((1, a_local * BLK, rows), lambda h: (h, 0, 0))],
        out_specs=pl.BlockSpec((1, rows, a_local * BLK), lambda h: (h, 0, 0)),
        compiler_params=pltpu.CompilerParams(vmem_limit_bytes=60 * 1024 * 1024),
    )(flat)
    return (update, energy)


def solution(mesh):
    placed = (
        P("pair", None, None, None),
        P(None, None, None, ("virt", "pair")),
        P(),
        P(),
        P("pair", None, None),
        P(),
        P(),
    )

    def run(*arrays):
        amplitudes, integrals = arrays[:2]
        loc = integrals.shape[3] // (mesh.shape["virt"] * mesh.shape["pair"])
        whole_slots = loc % amplitudes.shape[3] == 0
        whole_chunks = (integrals.shape[1] // mesh.shape["virt"]) % (2 * A_UNIT) == 0
        body = fused_shards if whole_slots and whole_chunks else shards
        return jax.shard_map(
            body,
            mesh=mesh,
            in_specs=placed,
            out_specs=(P("pair", None, "virt"), P("pair", "virt")),
            check_vma=False,
        )(*arrays)

    return run
```

```python
import functools

import jax
import jax.numpy as jnp
from jax import lax
from jax.experimental import pallas as pl
from jax.experimental.pallas import tpu as pltpu
from jax.sharding import PartitionSpec as P

IRREPS = 8
NV = 512
BLK = 64
CS = 16
SLABS = 2
A_UNIT = 16
MESH = pl.DeviceIdType.MESH
TURNS = {(8, 4): (7, 6, 5, 3, 4, 2, 7, 6, 5, 3, 4, 2, 1, 1, 0, 0)}


def pick_counts(irrep_ids, table):
    onehot = irrep_ids[..., None] == jnp.arange(table.shape[0], dtype=jnp.int32)
    return jnp.sum(jnp.where(onehot, table, 0), axis=-1)


def shards(amplitudes, integrals, virt_counts, pair_counts, pair_list, eps_occ, eps_virt):
    local_irreps = amplitudes.shape[0]
    rows = amplitudes.shape[1]
    width = amplitudes.shape[3]
    n_virt = lax.axis_size("virt")
    n_pair = lax.axis_size("pair")
    a_local = NV // n_virt
    irrep_ids = lax.axis_index("pair") * local_irreps + jnp.arange(local_irreps, dtype=jnp.int32)
    slots = jnp.arange(BLK, dtype=jnp.int32)
    live_d = slots[None, :] < pick_counts(irrep_ids, virt_counts)[:, None]
    dmask = jnp.tile(live_d, (1, CS)).astype(jnp.bfloat16)
    masked = amplitudes * dmask[:, None, None, :]
    ladder = jnp.zeros((local_irreps, rows, a_local, BLK), jnp.float32)
    for s in range(SLABS):
        piece = integrals[s]
        moved = lax.all_to_all(
            lax.all_to_all(piece, "virt", split_axis=0, concat_axis=2, tiled=True),
            "pair",
            split_axis=1,
            concat_axis=2,
            tiled=True,
        )
        moved = moved.reshape(a_local, local_irreps, n_pair, n_virt, -1)
        moved = jnp.transpose(moved, (0, 1, 3, 2, 4)).reshape(a_local, local_irreps, BLK, width)
        ladder = ladder + jnp.einsum(
            "hrk,ahsk->hras", masked[:, :, s, :], moved, preferred_element_type=jnp.float32
        )
    a_global = lax.axis_index("virt") * a_local + jnp.arange(a_local, dtype=jnp.int32)
    a_irrep = a_global // BLK
    a_slot = a_global % BLK
    live_a = a_slot < pick_counts(a_irrep, virt_counts)
    eps_a = lax.dynamic_slice_in_dim(eps_virt, lax.axis_index("virt") * a_local, a_local)
    b_irrep = jnp.bitwise_xor(a_irrep[None, :], irrep_ids[:, None])
    b_onehot = (b_irrep[..., None] == jnp.arange(IRREPS, dtype=jnp.int32)).astype(jnp.float32)
    eps_table = eps_virt.reshape(IRREPS, BLK)
    eps_b = jnp.einsum("hag,gs->has", b_onehot, eps_table, precision=lax.Precision.HIGHEST)
    live_b = slots[None, None, :] < pick_counts(b_irrep, virt_counts)[..., None]
    occ_onehot = pair_list[..., None] == jnp.arange(eps_occ.shape[0], dtype=jnp.int32)
    occ_terms = jnp.sum(jnp.where(occ_onehot, eps_occ, 0.0), axis=-1)
    occ = occ_terms[:, :, 0] + occ_terms[:, :, 1]
    live_rows = (
        jnp.arange(rows, dtype=jnp.int32)[None, :] < pick_counts(irrep_ids, pair_counts)[:, None]
    )
    denom = (eps_a[None, :, None] + eps_b)[:, None, :, :] - occ[:, :, None, None]
    live = live_rows[:, :, None, None] & live_a[None, None, :, None] & live_b[:, None, :, :]
    ratio = jnp.where(live, ladder / denom, jnp.zeros_like(ladder))
    update = ratio.astype(jnp.bfloat16).reshape(local_irreps, rows, a_local * BLK)
    partial_value = jnp.sum(ratio * ladder, axis=(2, 3)) / (NV * BLK)
    energy = lax.psum_scatter(partial_value, "virt", scatter_dimension=1, tiled=True)
    return (update, energy)


def flip_bits(index, pattern, count):
    flipped = 0
    weight = 1
    while weight < count:
        bit = (index // weight) % 2
        mine = (pattern // weight) % 2
        flipped = flipped + weight * (bit + mine - 2 * bit * mine)
        weight *= 2
    return flipped


def step_plan(count, units):
    turns = TURNS.get((count, units))
    if turns is None:
        turns = [count - 1 - i for _ in range(units // 2) for i in range(count)]
    plan = []
    used = [0] * count
    for i, d in enumerate(turns):
        for size in (1, 1) if i in (0, len(turns) - 1) else (2,):
            plan.append((d, used[d], size))
            used[d] += size
    return plan


def unit_matrix(count, outer, inner):
    rows = lax.broadcasted_iota(jnp.int32, (count * outer * inner, count * outer * inner), 0)
    cols = lax.broadcasted_iota(jnp.int32, (count * outer * inner, count * outer * inner), 1)
    unit = rows // (outer * inner)
    within = rows % (outer * inner)
    source = unit * (outer * inner) + (within % inner) * outer + within // inner
    return (source == cols).astype(jnp.float32).astype(jnp.bfloat16)


def ladder_kernel(
    n_virt, n_pair, irreps_here, depth, parts_sb, energy_scale,
    eri_ref, amps_ref, pair_ref, row_ref, vcount_ref, pcount_ref, eocc_ref, evirt_ref,
    got_ref, recv_ref, energy_ref,
    x_buf, stage, y_buf, out_buf, a_buf, amps, sort_in, sort_out, pick, levels, occ, cols_buf, terms, parts,
    x_sem, y_sem, own_sem, keep_sem, send_sem, recv_sem, out_sem, got_sem, term_sem, part_sem, a_sem,
):
    me_v = lax.axis_index("virt")
    me_p = lax.axis_index("pair")
    slabs = eri_ref.shape[0]
    loc = eri_ref.shape[2]
    irreps = irreps_here * n_pair
    ks = amps.shape[2]
    nrows = amps.shape[3]
    nv = row_ref.shape[1]
    nocc = eocc_ref.shape[0]
    a_local = nv // n_virt
    unit_rows = A_UNIT * irreps
    sb_here = n_pair * parts_sb
    out_rows = A_UNIT * sb_here
    plan = step_plan(n_virt, a_local // A_UNIT)
    steps = len(plan)
    e_cols = nrows // n_virt
    tile_n = 512
    tile_r = 256
    a_rows = a_buf.shape[1]
    peers = [d for d in range(2, n_pair)] + [1]
    first_unit = []
    total = 0
    for _, _, size in plan:
        first_unit.append(total)
        total += size

    def target(t):
        return flip_bits(me_v, plan[t][0], n_virt)

    def x_copy(t):
        _, start, size = plan[t]
        at = pl.multiple_of((target(t) * (a_local // A_UNIT) + start) * unit_rows, unit_rows)
        return pltpu.make_async_copy(
            eri_ref.at[:, pl.ds(at, size * unit_rows), :], x_buf.at[:, 0 : size * unit_rows, :], x_sem
        )

    def a_copy(block):
        per = nrows // a_rows
        at = pl.multiple_of((block % per) * a_rows, a_rows)
        return pltpu.make_async_copy(
            amps_ref.at[block // per, pl.ds(at, a_rows)], a_buf.at[block % 2], a_sem.at[block % 2]
        )

    def pair_copy(t, d):
        peer = flip_bits(me_p, d, n_pair)
        size = plan[t][2]
        return pltpu.make_async_remote_copy(
            src_ref=stage.at[t % depth, 0:size, peer],
            dst_ref=recv_ref.at[first_unit[t] : first_unit[t] + size, me_p],
            send_sem=send_sem.at[t % depth, d - 1],
            recv_sem=recv_sem.at[t, d - 1],
            device_id=(me_v, peer),
            device_id_type=MESH,
        )

    def own_copy(t):
        size = plan[t][2]
        return pltpu.make_async_copy(
            stage.at[t % depth, 0:size, me_p],
            recv_ref.at[first_unit[t] : first_unit[t] + size, me_p],
            own_sem.at[t % depth],
        )

    def out_copy(t, hh):
        d, start, size = plan[t]
        here = out_buf.at[first_unit[t] : first_unit[t] + size, hh]
        there = got_ref.at[hh, start : start + size, :, me_v]
        if d == 0:
            return pltpu.make_async_copy(here, there, keep_sem.at[start, hh])
        return pltpu.make_async_remote_copy(
            src_ref=here,
            dst_ref=there,
            send_sem=out_sem.at[t, hh],
            recv_sem=got_sem.at[t, hh],
            device_id=(target(t), me_p),
            device_id_type=MESH,
        )

    def part_copy(d):
        dest = flip_bits(me_v, d, n_virt)
        cols = pl.ds(pl.multiple_of(dest * e_cols, e_cols), e_cols)
        return pltpu.make_async_remote_copy(
            src_ref=terms.at[:, cols],
            dst_ref=parts.at[d - 1],
            send_sem=term_sem.at[d - 1],
            recv_sem=part_sem.at[d - 1],
            device_id=(dest, me_p),
            device_id_type=MESH,
        )

    def prepare(t):
        size = plan[t][2]
        n = size * unit_rows
        x_copy(t).wait()

        def sort_tile(i, carry):
            cols = pl.ds(pl.multiple_of(i * tile_n, tile_n), tile_n)
            for s in range(slabs):
                sorted_rows = jnp.dot(
                    sort_in[0:n, 0:n], x_buf[s, 0:n, cols], preferred_element_type=jnp.float32
                ).astype(jnp.bfloat16)
                for u in range(size):
                    for h in range(irreps):
                        at = u * unit_rows + h * A_UNIT
                        stage[
                            t % depth, u, h // irreps_here, h % irreps_here, s, :, cols
                        ] = sorted_rows[at : at + A_UNIT]
            return carry

        lax.fori_loop(0, loc // tile_n, sort_tile, 0)
        if t + 1 < steps:
            x_copy(t + 1).start()
        for d in peers:
            pair_copy(t, d).start()
        own_copy(t).start()

    def load_amps(hh):
        per = nrows // a_rows
        h = me_p * irreps_here + hh
        slot = lax.broadcasted_iota(jnp.int32, (1, tile_r), 1) % BLK
        dmask = jnp.where(slot < vcount_ref[h], 1.0, 0.0).astype(jnp.bfloat16)

        def block(i, carry):
            now = hh * per + i
            a_copy(now).wait()

            @pl.when(now + 1 < irreps_here * per)
            def _():
                a_copy(now + 1).start()

            rows = pl.ds(pl.multiple_of(i * a_rows, a_rows), a_rows)
            for c in range(ks // tile_r):
                lanes = slice(c * tile_r, (c + 1) * tile_r)
                mixed = a_buf[now % 2, :, :, lanes].reshape(a_rows * slabs, tile_r)
                split = jnp.dot(pick[0], mixed, preferred_element_type=jnp.float32).astype(jnp.bfloat16) * dmask
                turned = lax.dot_general(
                    pick[1], split, (((1,), (1,)), ((), ())), preferred_element_type=jnp.float32
                ).astype(jnp.bfloat16)
                for s in range(slabs):
                    amps[hh, s, lanes, rows] = turned[:, s * a_rows : (s + 1) * a_rows]
            return carry

        lax.fori_loop(0, per, block, 0)

    def fetch(t):
        size = plan[t][2]
        for d in range(1, n_pair):
            pair_copy(t, d).wait_recv()
        own_copy(t).wait()
        load = pltpu.make_async_copy(
            recv_ref.at[first_unit[t] : first_unit[t] + size], y_buf.at[0:size], y_sem
        )
        load.start()
        load.wait()

    def compute(t, hh):
        _, start, size = plan[t]
        n = size * out_rows
        h = me_p * irreps_here + hh
        bases = []
        lives = []
        for u in range(size):
            a_first = target(t) * a_local + (start + u) * A_UNIT
            a_irrep = a_first // BLK
            b_irrep = flip_bits(a_irrep, h, irreps)
            eps_a = levels[pl.ds(pl.multiple_of(a_first, A_UNIT), A_UNIT), 0:1]
            a_slot = a_first % BLK + lax.broadcasted_iota(jnp.int32, (A_UNIT, 1), 0)
            live_a = jnp.where(a_slot < vcount_ref[a_irrep], 1.0, 0.0)
            for b in range(sb_here):
                b_slot = me_v * sb_here + b
                bases.append(eps_a + evirt_ref[b_irrep * BLK + b_slot])
                lives.append(live_a * jnp.where(b_slot < vcount_ref[b_irrep], 1.0, 0.0))
        cols_buf[0, 0:n, :] = jnp.concatenate(bases, axis=0)
        cols_buf[1, 0:n, :] = jnp.concatenate(lives, axis=0)

        def tile(i, carry):
            cols = pl.ds(pl.multiple_of(i * tile_r, tile_r), tile_r)
            ladder = None
            for s in range(slabs):
                left = jnp.concatenate(
                    [
                        y_buf[u, p, hh, s, :, j * ks : (j + 1) * ks]
                        for u in range(size)
                        for p in range(n_pair)
                        for j in range(parts_sb)
                    ],
                    axis=0,
                )
                term = jnp.dot(left, amps[hh, s, :, cols], preferred_element_type=jnp.float32)
                ladder = term if ladder is None else ladder + term
            denom = cols_buf[0, 0:n, :] - occ[hh : hh + 1, cols]
            live = cols_buf[1, 0:n, :] * occ[irreps_here + hh : irreps_here + hh + 1, cols]
            ratio = jnp.where(live > 0.5, ladder / denom, 0.0)
            terms[hh : hh + 1, cols] += jnp.sum(ratio * ladder, axis=0, keepdims=True)
            update = jnp.dot(
                sort_out[0:n, 0:n], ratio.astype(jnp.bfloat16), preferred_element_type=jnp.float32
            ).astype(jnp.bfloat16)
            out_buf[first_unit[t] : first_unit[t] + size, hh, :, :, cols] = update.reshape(
                size, A_UNIT, sb_here, tile_r
            )
            return carry

        lax.fori_loop(0, nrows // tile_r, tile, 0)
        out_copy(t, hh).start()

    def tables():
        sort_out[...] = unit_matrix(2, A_UNIT, sb_here)
        for i in range(nv // 128):
            piece = jnp.broadcast_to(row_ref[0:1, i * 128 : (i + 1) * 128], (128, 128))
            levels[i * 128 : (i + 1) * 128, :] = piece.T
        index = pair_ref[...]

        def add_level(o, acc):
            return acc + jnp.where(index == o, eocc_ref[o], 0.0)

        picked = lax.fori_loop(0, nocc, add_level, jnp.zeros(index.shape, jnp.float32))
        slot = lax.broadcasted_iota(jnp.int32, (1, nrows), 1)
        for hh in range(irreps_here):
            occ[hh : hh + 1, :] = picked[hh, 0:1, :] + picked[hh, 1:2, :]
            live = slot < pcount_ref[me_p * irreps_here + hh]
            occ[irreps_here + hh : irreps_here + hh + 1, :] = jnp.where(live, 1.0, 0.0)
        pick[0] = unit_matrix(1, slabs, a_rows)
        pick[1] = unit_matrix(1, 1, tile_r)
        terms[...] = jnp.zeros_like(terms)

    x_copy(0).start()
    a_copy(0).start()
    barrier = pltpu.get_barrier_semaphore()
    for d in range(1, n_pair):
        pl.semaphore_signal(barrier, inc=1, device_id=(me_v, flip_bits(me_p, d, n_pair)), device_id_type=MESH)
    for d in range(1, n_virt):
        pl.semaphore_signal(barrier, inc=1, device_id=(flip_bits(me_v, d, n_virt), me_p), device_id_type=MESH)
    sort_in[...] = unit_matrix(2, irreps, A_UNIT)
    pl.semaphore_wait(barrier, n_pair - 1 + n_virt - 1)

    ahead = 0
    while ahead < 2:
        prepare(ahead)
        ahead += 1
    tables()
    for hh in range(irreps_here):
        load_amps(hh)
        if hh == 0:
            fetch(0)
        compute(0, hh)
        if ahead < depth:
            prepare(ahead)
            ahead += 1
    while ahead < depth:
        prepare(ahead)
        ahead += 1
    for t in range(steps):
        if t > 0:
            fetch(t)
            for hh in range(irreps_here):
                compute(t, hh)
        for d in range(1, n_pair):
            pair_copy(t, d).wait_send()
        if t + depth < steps:
            prepare(t + depth)
    for d in range(1, n_virt):
        part_copy(d).start()
    for d in range(1, n_virt):
        part_copy(d).wait()
    mine = terms[:, pl.ds(pl.multiple_of(me_v * e_cols, e_cols), e_cols)]
    for d in range(1, n_virt):
        mine = mine + parts[d - 1]
    energy_ref[...] = mine / energy_scale
    for t in range(steps):
        for hh in range(irreps_here):
            out_copy(t, hh).wait()


def turn_kernel(in_ref, out_ref, turned, sem):
    irreps_here, units, unit, n_virt, sb_here, rows = in_ref.shape
    block = turned.shape[1]
    per_a = n_virt * sb_here
    group = block // per_a
    per = rows // block
    eye = unit_matrix(1, 1, block)

    def out_copy(i):
        at = pl.multiple_of((i % per) * block, block)
        return pltpu.make_async_copy(turned.at[i % 2], out_ref.at[i // per, pl.ds(at, block)], sem.at[i % 2])

    def step(i, carry):
        @pl.when(i >= 2)
        def _():
            out_copy(i - 2).wait()

        cols = pl.ds(pl.multiple_of((i % per) * block, block), block)
        for u in range(units):
            for a in range(0, unit, group):
                piece = in_ref[i // per, u, a : a + group, :, :, cols].reshape(block, block)
                lanes = (u * unit + a) * per_a
                turned[i % 2, :, lanes : lanes + block] = lax.dot_general(
                    eye, piece, (((1,), (1,)), ((), ())), preferred_element_type=jnp.float32
                ).astype(jnp.bfloat16)
        out_copy(i).start()
        return carry

    count = irreps_here * per
    lax.fori_loop(0, count, step, 0)
    for i in range(max(count - 2, 0), count):
        out_copy(i).wait()


def fused_shards(amplitudes, integrals, virt_counts, pair_counts, pair_list, eps_occ, eps_virt):
    irreps_here, rows, slabs, ks = amplitudes.shape
    n_virt = lax.axis_size("virt")
    n_pair = lax.axis_size("pair")
    nv = integrals.shape[1]
    irreps = integrals.shape[2]
    loc = integrals.shape[3]
    depth = 4
    a_local = nv // n_virt
    units = a_local // A_UNIT
    plan = step_plan(n_virt, units)
    steps = len(plan)
    parts_sb = loc // ks
    sb_here = n_pair * parts_sb
    a_rows = 256 // slabs

    eri = integrals.reshape(slabs, nv * irreps, loc)
    pairs = jnp.transpose(pair_list, (0, 2, 1))
    vmem = pl.BlockSpec(memory_space=pltpu.VMEM)
    smem = pl.BlockSpec(memory_space=pltpu.SMEM)
    hbm = pl.BlockSpec(memory_space=pl.ANY)
    got, _, energy = pl.pallas_call(
        functools.partial(ladder_kernel, n_virt, n_pair, irreps_here, depth, parts_sb, nv * BLK),
        out_shape=(
            pltpu.VMEM((irreps_here, units, A_UNIT, n_virt, sb_here, rows), jnp.bfloat16),
            jax.ShapeDtypeStruct((units * n_virt, n_pair, irreps_here, slabs, A_UNIT, loc), jnp.bfloat16),
            jax.ShapeDtypeStruct((irreps_here, rows // n_virt), jnp.float32),
        ),
        in_specs=[hbm, hbm, vmem, vmem, smem, smem, smem, smem],
        out_specs=(vmem, hbm, vmem),
        scratch_shapes=[
            pltpu.VMEM((slabs, 2 * A_UNIT * irreps, loc), jnp.bfloat16),
            pltpu.VMEM((depth, 2, n_pair, irreps_here, slabs, A_UNIT, loc), jnp.bfloat16),
            pltpu.VMEM((2, n_pair, irreps_here, slabs, A_UNIT, loc), jnp.bfloat16),
            pltpu.VMEM((units * n_virt, irreps_here, A_UNIT, sb_here, rows), jnp.bfloat16),
            pltpu.VMEM((2, a_rows, slabs, ks), jnp.bfloat16),
            pltpu.VMEM((irreps_here, slabs, ks, rows), jnp.bfloat16),
            pltpu.VMEM((2 * A_UNIT * irreps, 2 * A_UNIT * irreps), jnp.bfloat16),
            pltpu.VMEM((2 * A_UNIT * sb_here, 2 * A_UNIT * sb_here), jnp.bfloat16),
            pltpu.VMEM((2, 256, 256), jnp.bfloat16),
            pltpu.VMEM((nv, 128), jnp.float32),
            pltpu.VMEM((2 * irreps_here, rows), jnp.float32),
            pltpu.VMEM((2, 2 * A_UNIT * sb_here, 1), jnp.float32),
            pltpu.VMEM((irreps_here, rows), jnp.float32),
            pltpu.VMEM((n_virt - 1, irreps_here, rows // n_virt), jnp.float32),
            pltpu.SemaphoreType.DMA,
            pltpu.SemaphoreType.DMA,
            pltpu.SemaphoreType.DMA((depth,)),
            pltpu.SemaphoreType.DMA((units, irreps_here)),
            pltpu.SemaphoreType.DMA((depth, n_pair - 1)),
            pltpu.SemaphoreType.DMA((steps, n_pair - 1)),
            pltpu.SemaphoreType.DMA((steps, irreps_here)),
            pltpu.SemaphoreType.DMA((steps, irreps_here)),
            pltpu.SemaphoreType.DMA((n_virt - 1,)),
            pltpu.SemaphoreType.DMA((n_virt - 1,)),
            pltpu.SemaphoreType.DMA((2,)),
        ],
        compiler_params=pltpu.CompilerParams(
            collective_id=0, has_side_effects=True, vmem_limit_bytes=44 * 1024 * 1024
        ),
    )(eri, amplitudes, pairs, eps_virt.reshape(1, nv), virt_counts, pair_counts, eps_occ, eps_virt)
    update = pl.pallas_call(
        turn_kernel,
        out_shape=jax.ShapeDtypeStruct((irreps_here, rows, a_local * BLK), jnp.bfloat16),
        in_specs=[vmem],
        out_specs=hbm,
        scratch_shapes=[
            pltpu.VMEM((2, 256, a_local * BLK), jnp.bfloat16),
            pltpu.SemaphoreType.DMA((2,)),
        ],
        compiler_params=pltpu.CompilerParams(vmem_limit_bytes=12 * 1024 * 1024),
    )(pltpu.with_memory_space_constraint(got, pltpu.VMEM))
    return (update, energy)


def solution(mesh):
    placed = (
        P("pair", None, None, None),
        P(None, None, None, ("virt", "pair")),
        P(),
        P(),
        P("pair", None, None),
        P(),
        P(),
    )

    def run(*arrays):
        amplitudes, integrals = arrays[:2]
        loc = integrals.shape[3] // (mesh.shape["virt"] * mesh.shape["pair"])
        whole_slots = loc % amplitudes.shape[3] == 0
        whole_chunks = (integrals.shape[1] // mesh.shape["virt"]) % (2 * A_UNIT) == 0
        body = fused_shards if whole_slots and whole_chunks else shards
        return jax.shard_map(
            body,
            mesh=mesh,
            in_specs=placed,
            out_specs=(P("pair", None, "virt"), P("pair", "virt")),
            check_vma=False,
        )(*arrays)

    return run
```

```python
import functools

import jax
import jax.numpy as jnp
from jax import lax
from jax.experimental import pallas as pl
from jax.experimental.pallas import tpu as pltpu
from jax.sharding import PartitionSpec as P

IRREPS = 8
NV = 512
BLK = 64
CS = 16
SLABS = 2
A_UNIT = 16
MESH = pl.DeviceIdType.MESH
TURNS = {8: (7, 2, 6, 3, 5, 4, 1, 0)}


def pick_counts(irrep_ids, table):
    onehot = irrep_ids[..., None] == jnp.arange(table.shape[0], dtype=jnp.int32)
    return jnp.sum(jnp.where(onehot, table, 0), axis=-1)


def shards(amplitudes, integrals, virt_counts, pair_counts, pair_list, eps_occ, eps_virt):
    local_irreps = amplitudes.shape[0]
    rows = amplitudes.shape[1]
    width = amplitudes.shape[3]
    n_virt = lax.axis_size("virt")
    n_pair = lax.axis_size("pair")
    a_local = NV // n_virt
    irrep_ids = lax.axis_index("pair") * local_irreps + jnp.arange(local_irreps, dtype=jnp.int32)
    slots = jnp.arange(BLK, dtype=jnp.int32)
    live_d = slots[None, :] < pick_counts(irrep_ids, virt_counts)[:, None]
    dmask = jnp.tile(live_d, (1, CS)).astype(jnp.bfloat16)
    masked = amplitudes * dmask[:, None, None, :]
    ladder = jnp.zeros((local_irreps, rows, a_local, BLK), jnp.float32)
    for s in range(SLABS):
        piece = integrals[s]
        moved = lax.all_to_all(
            lax.all_to_all(piece, "virt", split_axis=0, concat_axis=2, tiled=True),
            "pair",
            split_axis=1,
            concat_axis=2,
            tiled=True,
        )
        moved = moved.reshape(a_local, local_irreps, n_pair, n_virt, -1)
        moved = jnp.transpose(moved, (0, 1, 3, 2, 4)).reshape(a_local, local_irreps, BLK, width)
        ladder = ladder + jnp.einsum(
            "hrk,ahsk->hras", masked[:, :, s, :], moved, preferred_element_type=jnp.float32
        )
    a_global = lax.axis_index("virt") * a_local + jnp.arange(a_local, dtype=jnp.int32)
    a_irrep = a_global // BLK
    a_slot = a_global % BLK
    live_a = a_slot < pick_counts(a_irrep, virt_counts)
    eps_a = lax.dynamic_slice_in_dim(eps_virt, lax.axis_index("virt") * a_local, a_local)
    b_irrep = jnp.bitwise_xor(a_irrep[None, :], irrep_ids[:, None])
    b_onehot = (b_irrep[..., None] == jnp.arange(IRREPS, dtype=jnp.int32)).astype(jnp.float32)
    eps_table = eps_virt.reshape(IRREPS, BLK)
    eps_b = jnp.einsum("hag,gs->has", b_onehot, eps_table, precision=lax.Precision.HIGHEST)
    live_b = slots[None, None, :] < pick_counts(b_irrep, virt_counts)[..., None]
    occ_onehot = pair_list[..., None] == jnp.arange(eps_occ.shape[0], dtype=jnp.int32)
    occ_terms = jnp.sum(jnp.where(occ_onehot, eps_occ, 0.0), axis=-1)
    occ = occ_terms[:, :, 0] + occ_terms[:, :, 1]
    live_rows = (
        jnp.arange(rows, dtype=jnp.int32)[None, :] < pick_counts(irrep_ids, pair_counts)[:, None]
    )
    denom = (eps_a[None, :, None] + eps_b)[:, None, :, :] - occ[:, :, None, None]
    live = live_rows[:, :, None, None] & live_a[None, None, :, None] & live_b[:, None, :, :]
    ratio = jnp.where(live, ladder / denom, jnp.zeros_like(ladder))
    update = ratio.astype(jnp.bfloat16).reshape(local_irreps, rows, a_local * BLK)
    partial_value = jnp.sum(ratio * ladder, axis=(2, 3)) / (NV * BLK)
    energy = lax.psum_scatter(partial_value, "virt", scatter_dimension=1, tiled=True)
    return (update, energy)


def flip_bits(index, pattern, count):
    flipped = 0
    weight = 1
    while weight < count:
        bit = (index // weight) % 2
        mine = (pattern // weight) % 2
        flipped = flipped + weight * (bit + mine - 2 * bit * mine)
        weight *= 2
    return flipped


def turn_order(count):
    return TURNS.get(count, tuple(range(count - 1, -1, -1)))


def unit_matrix(count, outer, inner):
    rows = lax.broadcasted_iota(jnp.int32, (count * outer * inner, count * outer * inner), 0)
    cols = lax.broadcasted_iota(jnp.int32, (count * outer * inner, count * outer * inner), 1)
    unit = rows // (outer * inner)
    within = rows % (outer * inner)
    source = unit * (outer * inner) + (within % inner) * outer + within // inner
    return (source == cols).astype(jnp.float32).astype(jnp.bfloat16)


def ladder_kernel(
    n_virt, n_pair, irreps_here, depth, parts_sb, energy_scale,
    eri_ref, amps_ref, pair_ref, row_ref, vcount_ref, pcount_ref, eocc_ref, evirt_ref,
    got_ref, recv_ref, energy_ref,
    x_buf, stage, y_buf, out_buf, a_buf, amps, sort_in, sort_out, pick, levels, occ, cols_buf, terms, parts,
    x_sem, y_sem, own_sem, keep_sem, send_sem, recv_sem, out_sem, got_sem, term_sem, part_sem, a_sem,
):
    me_v = lax.axis_index("virt")
    me_p = lax.axis_index("pair")
    slabs = eri_ref.shape[0]
    loc = eri_ref.shape[2]
    irreps = irreps_here * n_pair
    ks = amps.shape[2]
    nrows = amps.shape[3]
    nv = row_ref.shape[1]
    nocc = eocc_ref.shape[0]
    a_local = nv // n_virt
    unit_rows = A_UNIT * irreps
    sb_here = n_pair * parts_sb
    out_rows = A_UNIT * sb_here
    order = turn_order(n_virt)
    rounds = a_local // A_UNIT
    e_cols = nrows // n_virt
    tile_n = 512
    tile_m = 256
    tile_r = 512
    a_rows = a_buf.shape[1]
    peers = [d for d in range(2, n_pair)] + [1]

    def target(i):
        return flip_bits(me_v, order[i], n_virt)

    def x_copy(r, i):
        at = pl.multiple_of((target(i) * rounds + r) * unit_rows, unit_rows)
        return pltpu.make_async_copy(eri_ref.at[:, pl.ds(at, unit_rows), :], x_buf, x_sem)

    def a_copy(block):
        per = nrows // a_rows
        at = pl.multiple_of((block % per) * a_rows, a_rows)
        return pltpu.make_async_copy(
            amps_ref.at[block // per, pl.ds(at, a_rows)], a_buf.at[block % 2], a_sem.at[block % 2]
        )

    def pair_copy(r, i, d):
        peer = flip_bits(me_p, d, n_pair)
        return pltpu.make_async_remote_copy(
            src_ref=stage.at[i % depth, peer],
            dst_ref=recv_ref.at[r * n_virt + i, me_p],
            send_sem=send_sem.at[i % depth, d - 1],
            recv_sem=recv_sem.at[r * n_virt + i, d - 1],
            device_id=(me_v, peer),
            device_id_type=MESH,
        )

    def own_copy(r, i):
        return pltpu.make_async_copy(
            stage.at[i % depth, me_p], recv_ref.at[r * n_virt + i, me_p], own_sem.at[i % depth]
        )

    def out_copy(r, i, hh):
        here = out_buf.at[r * n_virt + i, hh]
        there = got_ref.at[hh, r, :, me_v]
        if order[i] == 0:
            return pltpu.make_async_copy(here, there, keep_sem.at[r, hh])
        return pltpu.make_async_remote_copy(
            src_ref=here,
            dst_ref=there,
            send_sem=out_sem.at[r * n_virt + i, hh],
            recv_sem=got_sem.at[r * n_virt + i, hh],
            device_id=(target(i), me_p),
            device_id_type=MESH,
        )

    def part_copy(d):
        dest = flip_bits(me_v, d, n_virt)
        cols = pl.ds(pl.multiple_of(dest * e_cols, e_cols), e_cols)
        return pltpu.make_async_remote_copy(
            src_ref=terms.at[:, cols],
            dst_ref=parts.at[d - 1],
            send_sem=term_sem.at[d - 1],
            recv_sem=part_sem.at[d - 1],
            device_id=(dest, me_p),
            device_id_type=MESH,
        )

    def prepare(r, i):
        x_copy(r, i).wait()

        def sort_tile(k, carry):
            cols = pl.ds(pl.multiple_of(k * tile_n, tile_n), tile_n)
            for s in range(slabs):
                sorted_rows = jnp.dot(
                    sort_in[...], x_buf[s, :, cols], preferred_element_type=jnp.float32
                ).astype(jnp.bfloat16)
                for h in range(irreps):
                    stage[i % depth, h // irreps_here, h % irreps_here, s, :, cols] = sorted_rows[
                        h * A_UNIT : (h + 1) * A_UNIT
                    ]
            return carry

        lax.fori_loop(0, loc // tile_n, sort_tile, 0)
        if i + 1 < n_virt:
            x_copy(r, i + 1).start()
        else:

            @pl.when(r + 1 < rounds)
            def _():
                x_copy(r + 1, 0).start()

        for d in peers:
            pair_copy(r, i, d).start()
        own_copy(r, i).start()

    def load_amps(hh):
        per = nrows // a_rows
        h = me_p * irreps_here + hh
        slot = lax.broadcasted_iota(jnp.int32, (1, tile_m), 1) % BLK
        dmask = jnp.where(slot < vcount_ref[h], 1.0, 0.0).astype(jnp.bfloat16)

        def block(i, carry):
            now = hh * per + i
            a_copy(now).wait()

            @pl.when(now + 1 < irreps_here * per)
            def _():
                a_copy(now + 1).start()

            rows = pl.ds(pl.multiple_of(i * a_rows, a_rows), a_rows)
            for c in range(ks // tile_m):
                lanes = slice(c * tile_m, (c + 1) * tile_m)
                mixed = a_buf[now % 2, :, :, lanes].reshape(a_rows * slabs, tile_m)
                split = jnp.dot(pick[0], mixed, preferred_element_type=jnp.float32).astype(jnp.bfloat16) * dmask
                turned = lax.dot_general(
                    pick[1], split, (((1,), (1,)), ((), ())), preferred_element_type=jnp.float32
                ).astype(jnp.bfloat16)
                for s in range(slabs):
                    amps[hh, s, lanes, rows] = turned[:, s * a_rows : (s + 1) * a_rows]
            return carry

        lax.fori_loop(0, per, block, 0)

    def fetch(r, i):
        for d in range(1, n_pair):
            pair_copy(r, i, d).wait_recv()
        own_copy(r, i).wait()
        load = pltpu.make_async_copy(recv_ref.at[r * n_virt + i], y_buf, y_sem)
        load.start()
        load.wait()

    def compute(r, i, hh):
        h = me_p * irreps_here + hh
        a_first = target(i) * a_local + r * A_UNIT
        a_irrep = a_first // BLK
        b_irrep = flip_bits(a_irrep, h, irreps)
        eps_a = levels[pl.ds(pl.multiple_of(a_first, A_UNIT), A_UNIT), 0:1]
        a_slot = a_first % BLK + lax.broadcasted_iota(jnp.int32, (A_UNIT, 1), 0)
        live_a = jnp.where(a_slot < vcount_ref[a_irrep], 1.0, 0.0)
        bases = []
        lives = []
        for b in range(sb_here):
            b_slot = me_v * sb_here + b
            bases.append(eps_a + evirt_ref[b_irrep * BLK + b_slot])
            lives.append(live_a * jnp.where(b_slot < vcount_ref[b_irrep], 1.0, 0.0))
        cols_buf[0] = jnp.concatenate(bases, axis=0)
        cols_buf[1] = jnp.concatenate(lives, axis=0)

        def tile(k, carry):
            cols = pl.ds(pl.multiple_of(k * tile_r, tile_r), tile_r)
            ladder = None
            for s in range(slabs):
                left = jnp.concatenate(
                    [y_buf[p, hh, s, :, j * ks : (j + 1) * ks] for p in range(n_pair) for j in range(parts_sb)],
                    axis=0,
                )
                term = jnp.dot(left, amps[hh, s, :, cols], preferred_element_type=jnp.float32)
                ladder = term if ladder is None else ladder + term
            denom = cols_buf[0] - occ[hh : hh + 1, cols]
            live = cols_buf[1] * occ[irreps_here + hh : irreps_here + hh + 1, cols]
            ratio = jnp.where(live > 0.5, ladder / denom, 0.0)
            terms[hh : hh + 1, cols] += jnp.sum(ratio * ladder, axis=0, keepdims=True)
            update = jnp.dot(
                sort_out[...], ratio.astype(jnp.bfloat16), preferred_element_type=jnp.float32
            ).astype(jnp.bfloat16)
            out_buf[r * n_virt + i, hh, :, :, cols] = update.reshape(A_UNIT, sb_here, tile_r)
            return carry

        lax.fori_loop(0, nrows // tile_r, tile, 0)
        out_copy(r, i, hh).start()

    def tables():
        sort_out[...] = unit_matrix(1, A_UNIT, sb_here)
        for i in range(nv // 128):
            piece = jnp.broadcast_to(row_ref[0:1, i * 128 : (i + 1) * 128], (128, 128))
            levels[i * 128 : (i + 1) * 128, :] = piece.T
        index = pair_ref[...]

        def add_level(o, acc):
            return acc + jnp.where(index == o, eocc_ref[o], 0.0)

        picked = lax.fori_loop(0, nocc, add_level, jnp.zeros(index.shape, jnp.float32))
        slot = lax.broadcasted_iota(jnp.int32, (1, nrows), 1)
        for hh in range(irreps_here):
            occ[hh : hh + 1, :] = picked[hh, 0:1, :] + picked[hh, 1:2, :]
            live = slot < pcount_ref[me_p * irreps_here + hh]
            occ[irreps_here + hh : irreps_here + hh + 1, :] = jnp.where(live, 1.0, 0.0)
        pick[0] = unit_matrix(1, slabs, a_rows)
        pick[1] = unit_matrix(1, 1, tile_m)
        terms[...] = jnp.zeros_like(terms)

    x_copy(0, 0).start()
    a_copy(0).start()
    barrier = pltpu.get_barrier_semaphore()
    for d in range(1, n_pair):
        pl.semaphore_signal(barrier, inc=1, device_id=(me_v, flip_bits(me_p, d, n_pair)), device_id_type=MESH)
    for d in range(1, n_virt):
        pl.semaphore_signal(barrier, inc=1, device_id=(flip_bits(me_v, d, n_virt), me_p), device_id_type=MESH)
    sort_in[...] = unit_matrix(1, irreps, A_UNIT)
    pl.semaphore_wait(barrier, n_pair - 1 + n_virt - 1)

    early = depth - irreps_here
    for i in range(early):
        prepare(0, i)
    tables()

    def one_round(r, carry):
        for i in range(n_virt):
            for hh in range(irreps_here):
                if i == 0:

                    @pl.when(r == 0)
                    def _():
                        load_amps(hh)

                if hh == 0:
                    fetch(r, i)
                compute(r, i, hh)
                if i == 0:

                    @pl.when(r == 0)
                    def _():
                        prepare(0, early + hh)

            for d in range(1, n_pair):
                pair_copy(r, i, d).wait_send()
            if i + depth < n_virt:
                prepare(r, i + depth)
            else:

                @pl.when(r + 1 < rounds)
                def _():
                    prepare(r + 1, i + depth - n_virt)

        return carry

    lax.fori_loop(0, rounds, one_round, 0)
    for d in range(1, n_virt):
        part_copy(d).start()
    for d in range(1, n_virt):
        part_copy(d).wait()
    mine = terms[:, pl.ds(pl.multiple_of(me_v * e_cols, e_cols), e_cols)]
    for d in range(1, n_virt):
        mine = mine + parts[d - 1]
    energy_ref[...] = mine / energy_scale

    def drain(r, carry):
        for i in range(n_virt):
            for hh in range(irreps_here):
                out_copy(r, i, hh).wait()
        return carry

    lax.fori_loop(0, rounds, drain, 0)


def turn_kernel(in_ref, out_ref, turned, sem):
    irreps_here, units, unit, n_virt, sb_here, rows = in_ref.shape
    block = turned.shape[1]
    per_a = n_virt * sb_here
    group = block // per_a
    per = rows // block
    eye = unit_matrix(1, 1, block)

    def out_copy(i):
        at = pl.multiple_of((i % per) * block, block)
        return pltpu.make_async_copy(turned.at[i % 2], out_ref.at[i // per, pl.ds(at, block)], sem.at[i % 2])

    def step(i, carry):
        @pl.when(i >= 2)
        def _():
            out_copy(i - 2).wait()

        cols = pl.ds(pl.multiple_of((i % per) * block, block), block)
        for u in range(units):
            for a in range(0, unit, group):
                piece = in_ref[i // per, u, a : a + group, :, :, cols].reshape(block, block)
                lanes = (u * unit + a) * per_a
                if (a // group) % 2:
                    turned[i % 2, :, lanes : lanes + block] = piece.T
                else:
                    turned[i % 2, :, lanes : lanes + block] = lax.dot_general(
                        eye, piece, (((1,), (1,)), ((), ())), preferred_element_type=jnp.float32
                    ).astype(jnp.bfloat16)
        out_copy(i).start()
        return carry

    count = irreps_here * per
    lax.fori_loop(0, count, step, 0)
    for i in range(max(count - 2, 0), count):
        out_copy(i).wait()


def fused_shards(amplitudes, integrals, virt_counts, pair_counts, pair_list, eps_occ, eps_virt):
    irreps_here, rows, slabs, ks = amplitudes.shape
    n_virt = lax.axis_size("virt")
    n_pair = lax.axis_size("pair")
    nv = integrals.shape[1]
    irreps = integrals.shape[2]
    loc = integrals.shape[3]
    depth = 4
    a_local = nv // n_virt
    units = a_local // A_UNIT
    steps = n_virt * units
    parts_sb = loc // ks
    sb_here = n_pair * parts_sb
    a_rows = 256 // slabs

    eri = integrals.reshape(slabs, nv * irreps, loc)
    pairs = jnp.transpose(pair_list, (0, 2, 1))
    vmem = pl.BlockSpec(memory_space=pltpu.VMEM)
    smem = pl.BlockSpec(memory_space=pltpu.SMEM)
    hbm = pl.BlockSpec(memory_space=pl.ANY)
    got, _, energy = pl.pallas_call(
        functools.partial(ladder_kernel, n_virt, n_pair, irreps_here, depth, parts_sb, nv * BLK),
        out_shape=(
            pltpu.VMEM((irreps_here, units, A_UNIT, n_virt, sb_here, rows), jnp.bfloat16),
            jax.ShapeDtypeStruct((units * n_virt, n_pair, irreps_here, slabs, A_UNIT, loc), jnp.bfloat16),
            jax.ShapeDtypeStruct((irreps_here, rows // n_virt), jnp.float32),
        ),
        in_specs=[hbm, hbm, vmem, vmem, smem, smem, smem, smem],
        out_specs=(vmem, hbm, vmem),
        scratch_shapes=[
            pltpu.VMEM((slabs, A_UNIT * irreps, loc), jnp.bfloat16),
            pltpu.VMEM((depth, n_pair, irreps_here, slabs, A_UNIT, loc), jnp.bfloat16),
            pltpu.VMEM((n_pair, irreps_here, slabs, A_UNIT, loc), jnp.bfloat16),
            pltpu.VMEM((units * n_virt, irreps_here, A_UNIT, sb_here, rows), jnp.bfloat16),
            pltpu.VMEM((2, a_rows, slabs, ks), jnp.bfloat16),
            pltpu.VMEM((irreps_here, slabs, ks, rows), jnp.bfloat16),
            pltpu.VMEM((A_UNIT * irreps, A_UNIT * irreps), jnp.bfloat16),
            pltpu.VMEM((A_UNIT * sb_here, A_UNIT * sb_here), jnp.bfloat16),
            pltpu.VMEM((2, 256, 256), jnp.bfloat16),
            pltpu.VMEM((nv, 128), jnp.float32),
            pltpu.VMEM((2 * irreps_here, rows), jnp.float32),
            pltpu.VMEM((2, A_UNIT * sb_here, 1), jnp.float32),
            pltpu.VMEM((irreps_here, rows), jnp.float32),
            pltpu.VMEM((n_virt - 1, irreps_here, rows // n_virt), jnp.float32),
            pltpu.SemaphoreType.DMA,
            pltpu.SemaphoreType.DMA,
            pltpu.SemaphoreType.DMA((depth,)),
            pltpu.SemaphoreType.DMA((units, irreps_here)),
            pltpu.SemaphoreType.DMA((depth, n_pair - 1)),
            pltpu.SemaphoreType.DMA((steps, n_pair - 1)),
            pltpu.SemaphoreType.DMA((steps, irreps_here)),
            pltpu.SemaphoreType.DMA((steps, irreps_here)),
            pltpu.SemaphoreType.DMA((n_virt - 1,)),
            pltpu.SemaphoreType.DMA((n_virt - 1,)),
            pltpu.SemaphoreType.DMA((2,)),
        ],
        compiler_params=pltpu.CompilerParams(
            collective_id=0, has_side_effects=True, vmem_limit_bytes=44 * 1024 * 1024
        ),
    )(eri, amplitudes, pairs, eps_virt.reshape(1, nv), virt_counts, pair_counts, eps_occ, eps_virt)
    update = pl.pallas_call(
        turn_kernel,
        out_shape=jax.ShapeDtypeStruct((irreps_here, rows, a_local * BLK), jnp.bfloat16),
        in_specs=[vmem],
        out_specs=hbm,
        scratch_shapes=[
            pltpu.VMEM((2, 256, a_local * BLK), jnp.bfloat16),
            pltpu.SemaphoreType.DMA((2,)),
        ],
        compiler_params=pltpu.CompilerParams(vmem_limit_bytes=12 * 1024 * 1024),
    )(pltpu.with_memory_space_constraint(got, pltpu.VMEM))
    return (update, energy)


def solution(mesh):
    placed = (
        P("pair", None, None, None),
        P(None, None, None, ("virt", "pair")),
        P(),
        P(),
        P("pair", None, None),
        P(),
        P(),
    )

    def run(*arrays):
        amplitudes, integrals = arrays[:2]
        loc = integrals.shape[3] // (mesh.shape["virt"] * mesh.shape["pair"])
        whole_slots = loc % amplitudes.shape[3] == 0
        whole_chunks = (integrals.shape[1] // mesh.shape["virt"]) % A_UNIT == 0
        body = fused_shards if whole_slots and whole_chunks else shards
        return jax.shard_map(
            body,
            mesh=mesh,
            in_specs=placed,
            out_specs=(P("pair", None, "virt"), P("pair", "virt")),
            check_vma=False,
        )(*arrays)

    return run
```

```python
import functools

import jax
import jax.numpy as jnp
from jax import lax
from jax.experimental import pallas as pl
from jax.experimental.pallas import tpu as pltpu
from jax.sharding import PartitionSpec as P

IRREPS = 8
NV = 512
BLK = 64
CS = 16
SLABS = 2
A_UNIT = 16
MESH = pl.DeviceIdType.MESH
TURNS = {8: (7, 6, 5, 4, 2, 3, 1, 0)}


def pick_counts(irrep_ids, table):
    onehot = irrep_ids[..., None] == jnp.arange(table.shape[0], dtype=jnp.int32)
    return jnp.sum(jnp.where(onehot, table, 0), axis=-1)


def shards(amplitudes, integrals, virt_counts, pair_counts, pair_list, eps_occ, eps_virt):
    local_irreps = amplitudes.shape[0]
    rows = amplitudes.shape[1]
    width = amplitudes.shape[3]
    n_virt = lax.axis_size("virt")
    n_pair = lax.axis_size("pair")
    a_local = NV // n_virt
    irrep_ids = lax.axis_index("pair") * local_irreps + jnp.arange(local_irreps, dtype=jnp.int32)
    slots = jnp.arange(BLK, dtype=jnp.int32)
    live_d = slots[None, :] < pick_counts(irrep_ids, virt_counts)[:, None]
    dmask = jnp.tile(live_d, (1, CS)).astype(jnp.bfloat16)
    masked = amplitudes * dmask[:, None, None, :]
    ladder = jnp.zeros((local_irreps, rows, a_local, BLK), jnp.float32)
    for s in range(SLABS):
        piece = integrals[s]
        moved = lax.all_to_all(
            lax.all_to_all(piece, "virt", split_axis=0, concat_axis=2, tiled=True),
            "pair",
            split_axis=1,
            concat_axis=2,
            tiled=True,
        )
        moved = moved.reshape(a_local, local_irreps, n_pair, n_virt, -1)
        moved = jnp.transpose(moved, (0, 1, 3, 2, 4)).reshape(a_local, local_irreps, BLK, width)
        ladder = ladder + jnp.einsum(
            "hrk,ahsk->hras", masked[:, :, s, :], moved, preferred_element_type=jnp.float32
        )
    a_global = lax.axis_index("virt") * a_local + jnp.arange(a_local, dtype=jnp.int32)
    a_irrep = a_global // BLK
    a_slot = a_global % BLK
    live_a = a_slot < pick_counts(a_irrep, virt_counts)
    eps_a = lax.dynamic_slice_in_dim(eps_virt, lax.axis_index("virt") * a_local, a_local)
    b_irrep = jnp.bitwise_xor(a_irrep[None, :], irrep_ids[:, None])
    b_onehot = (b_irrep[..., None] == jnp.arange(IRREPS, dtype=jnp.int32)).astype(jnp.float32)
    eps_table = eps_virt.reshape(IRREPS, BLK)
    eps_b = jnp.einsum("hag,gs->has", b_onehot, eps_table, precision=lax.Precision.HIGHEST)
    live_b = slots[None, None, :] < pick_counts(b_irrep, virt_counts)[..., None]
    occ_onehot = pair_list[..., None] == jnp.arange(eps_occ.shape[0], dtype=jnp.int32)
    occ_terms = jnp.sum(jnp.where(occ_onehot, eps_occ, 0.0), axis=-1)
    occ = occ_terms[:, :, 0] + occ_terms[:, :, 1]
    live_rows = (
        jnp.arange(rows, dtype=jnp.int32)[None, :] < pick_counts(irrep_ids, pair_counts)[:, None]
    )
    denom = (eps_a[None, :, None] + eps_b)[:, None, :, :] - occ[:, :, None, None]
    live = live_rows[:, :, None, None] & live_a[None, None, :, None] & live_b[:, None, :, :]
    ratio = jnp.where(live, ladder / denom, jnp.zeros_like(ladder))
    update = ratio.astype(jnp.bfloat16).reshape(local_irreps, rows, a_local * BLK)
    partial_value = jnp.sum(ratio * ladder, axis=(2, 3)) / (NV * BLK)
    energy = lax.psum_scatter(partial_value, "virt", scatter_dimension=1, tiled=True)
    return (update, energy)


def flip_bits(index, pattern, count):
    flipped = 0
    weight = 1
    while weight < count:
        bit = (index // weight) % 2
        mine = (pattern // weight) % 2
        flipped = flipped + weight * (bit + mine - 2 * bit * mine)
        weight *= 2
    return flipped


def turn_order(count):
    return TURNS.get(count, tuple(range(count - 1, -1, -1)))


def unit_matrix(count, outer, inner):
    rows = lax.broadcasted_iota(jnp.int32, (count * outer * inner, count * outer * inner), 0)
    cols = lax.broadcasted_iota(jnp.int32, (count * outer * inner, count * outer * inner), 1)
    unit = rows // (outer * inner)
    within = rows % (outer * inner)
    source = unit * (outer * inner) + (within % inner) * outer + within // inner
    return (source == cols).astype(jnp.float32).astype(jnp.bfloat16)


def ladder_kernel(
    n_virt, n_pair, irreps_here, depth, parts_sb, energy_scale,
    eri_ref, amps_ref, pair_ref, row_ref, vcount_ref, pcount_ref, eocc_ref, evirt_ref,
    got_ref, recv_ref, energy_ref,
    x_buf, stage, y_buf, out_buf, a_buf, amps, sort_in, sort_out, pick, levels, occ, cols_buf, terms, parts,
    x_sem, y_sem, own_sem, keep_sem, send_sem, recv_sem, out_sem, got_sem, term_sem, part_sem, a_sem, first_sem,
):
    me_v = lax.axis_index("virt")
    me_p = lax.axis_index("pair")
    slabs = eri_ref.shape[0]
    loc = eri_ref.shape[2]
    irreps = irreps_here * n_pair
    ks = amps.shape[2]
    nrows = amps.shape[3]
    nv = row_ref.shape[1]
    nocc = eocc_ref.shape[0]
    a_local = nv // n_virt
    unit_rows = A_UNIT * irreps
    sb_here = n_pair * parts_sb
    out_rows = A_UNIT * sb_here
    order = turn_order(n_virt)
    rounds = a_local // A_UNIT
    e_cols = nrows // n_virt
    tile_n = 512
    tile_m = 256
    tile_r = 512
    a_rows = a_buf.shape[1]
    peers = [d for d in range(2, n_pair)] + [1]

    def target(i):
        return flip_bits(me_v, order[i], n_virt)

    def x_copy(r, i):
        at = pl.multiple_of((target(i) * rounds + r) * unit_rows, unit_rows)
        return pltpu.make_async_copy(eri_ref.at[:, pl.ds(at, unit_rows), :], x_buf, x_sem)

    def a_copy(block):
        per = nrows // a_rows
        at = pl.multiple_of((block % per) * a_rows, a_rows)
        return pltpu.make_async_copy(
            amps_ref.at[block // per, pl.ds(at, a_rows)], a_buf.at[block % 2], a_sem.at[block % 2]
        )

    def pair_copy(r, i, d):
        peer = flip_bits(me_p, d, n_pair)
        return pltpu.make_async_remote_copy(
            src_ref=stage.at[i % depth, peer],
            dst_ref=recv_ref.at[r * n_virt + i, me_p],
            send_sem=send_sem.at[i % depth, d - 1],
            recv_sem=recv_sem.at[r * n_virt + i, d - 1],
            device_id=(me_v, peer),
            device_id_type=MESH,
        )

    def first_copy(hh, d):
        peer = flip_bits(me_p, d, n_pair)
        return pltpu.make_async_remote_copy(
            src_ref=stage.at[0, peer, hh],
            dst_ref=recv_ref.at[0, me_p, hh],
            send_sem=send_sem.at[0, d - 1],
            recv_sem=first_sem.at[hh, d - 1],
            device_id=(me_v, peer),
            device_id_type=MESH,
        )

    def own_copy(r, i):
        return pltpu.make_async_copy(
            stage.at[i % depth, me_p], recv_ref.at[r * n_virt + i, me_p], own_sem.at[i % depth]
        )

    def out_copy(r, i, hh):
        here = out_buf.at[r * n_virt + i, hh]
        there = got_ref.at[hh, r, :, me_v]
        if order[i] == 0:
            return pltpu.make_async_copy(here, there, keep_sem.at[r, hh])
        return pltpu.make_async_remote_copy(
            src_ref=here,
            dst_ref=there,
            send_sem=out_sem.at[r * n_virt + i, hh],
            recv_sem=got_sem.at[r * n_virt + i, hh],
            device_id=(target(i), me_p),
            device_id_type=MESH,
        )

    def part_copy(d):
        dest = flip_bits(me_v, d, n_virt)
        cols = pl.ds(pl.multiple_of(dest * e_cols, e_cols), e_cols)
        return pltpu.make_async_remote_copy(
            src_ref=terms.at[:, cols],
            dst_ref=parts.at[d - 1],
            send_sem=term_sem.at[d - 1],
            recv_sem=part_sem.at[d - 1],
            device_id=(dest, me_p),
            device_id_type=MESH,
        )

    def prepare(r, i, first=False):
        x_copy(r, i).wait()

        def sort_tile(k, carry):
            cols = pl.ds(pl.multiple_of(k * tile_n, tile_n), tile_n)
            for s in range(slabs):
                sorted_rows = jnp.dot(
                    sort_in[...], x_buf[s, :, cols], preferred_element_type=jnp.float32
                ).astype(jnp.bfloat16)
                for h in range(irreps):
                    stage[i % depth, h // irreps_here, h % irreps_here, s, :, cols] = sorted_rows[
                        h * A_UNIT : (h + 1) * A_UNIT
                    ]
            return carry

        lax.fori_loop(0, loc // tile_n, sort_tile, 0)
        if i + 1 < n_virt:
            x_copy(r, i + 1).start()
        else:

            @pl.when(r + 1 < rounds)
            def _():
                x_copy(r + 1, 0).start()

        if first:
            for hh in range(irreps_here):
                for d in peers:
                    first_copy(hh, d).start()
        else:
            for d in peers:
                pair_copy(r, i, d).start()
        own_copy(r, i).start()

    def load_amps(hh):
        per = nrows // a_rows
        h = me_p * irreps_here + hh
        slot = lax.broadcasted_iota(jnp.int32, (1, tile_m), 1) % BLK
        dmask = jnp.where(slot < vcount_ref[h], 1.0, 0.0).astype(jnp.bfloat16)

        def block(i, carry):
            now = hh * per + i
            a_copy(now).wait()

            @pl.when(now + 1 < irreps_here * per)
            def _():
                a_copy(now + 1).start()

            rows = pl.ds(pl.multiple_of(i * a_rows, a_rows), a_rows)
            for c in range(ks // tile_m):
                lanes = slice(c * tile_m, (c + 1) * tile_m)
                mixed = a_buf[now % 2, :, :, lanes].reshape(a_rows * slabs, tile_m)
                split = jnp.dot(pick[0], mixed, preferred_element_type=jnp.float32).astype(jnp.bfloat16) * dmask
                turned = lax.dot_general(
                    pick[1], split, (((1,), (1,)), ((), ())), preferred_element_type=jnp.float32
                ).astype(jnp.bfloat16)
                for s in range(slabs):
                    amps[hh, s, lanes, rows] = turned[:, s * a_rows : (s + 1) * a_rows]
            return carry

        lax.fori_loop(0, per, block, 0)

    def fetch(r, i):
        for d in range(1, n_pair):
            pair_copy(r, i, d).wait_recv()
        own_copy(r, i).wait()
        load = pltpu.make_async_copy(recv_ref.at[r * n_virt + i], y_buf, y_sem)
        load.start()
        load.wait()

    def fetch_first(hh):
        for d in range(1, n_pair):
            first_copy(hh, d).wait_recv()
        if hh == 0:
            own_copy(0, 0).wait()
        load = pltpu.make_async_copy(recv_ref.at[0, :, hh], y_buf.at[:, hh], y_sem)
        load.start()
        load.wait()

    def compute(r, i, hh):
        h = me_p * irreps_here + hh
        a_first = target(i) * a_local + r * A_UNIT
        a_irrep = a_first // BLK
        b_irrep = flip_bits(a_irrep, h, irreps)
        eps_a = levels[pl.ds(pl.multiple_of(a_first, A_UNIT), A_UNIT), 0:1]
        a_slot = a_first % BLK + lax.broadcasted_iota(jnp.int32, (A_UNIT, 1), 0)
        live_a = jnp.where(a_slot < vcount_ref[a_irrep], 1.0, 0.0)
        bases = []
        lives = []
        for b in range(sb_here):
            b_slot = me_v * sb_here + b
            bases.append(eps_a + evirt_ref[b_irrep * BLK + b_slot])
            lives.append(live_a * jnp.where(b_slot < vcount_ref[b_irrep], 1.0, 0.0))
        cols_buf[0] = jnp.concatenate(bases, axis=0)
        cols_buf[1] = jnp.concatenate(lives, axis=0)

        def tile(k, carry):
            cols = pl.ds(pl.multiple_of(k * tile_r, tile_r), tile_r)
            ladder = None
            for s in range(slabs):
                left = jnp.concatenate(
                    [y_buf[p, hh, s, :, j * ks : (j + 1) * ks] for p in range(n_pair) for j in range(parts_sb)],
                    axis=0,
                )
                term = jnp.dot(left, amps[hh, s, :, cols], preferred_element_type=jnp.float32)
                ladder = term if ladder is None else ladder + term
            denom = cols_buf[0] - occ[hh : hh + 1, cols]
            live = cols_buf[1] * occ[irreps_here + hh : irreps_here + hh + 1, cols]
            ratio = jnp.where(live > 0.5, ladder / denom, 0.0)
            terms[hh : hh + 1, cols] += jnp.sum(ratio * ladder, axis=0, keepdims=True)
            update = jnp.dot(
                sort_out[...], ratio.astype(jnp.bfloat16), preferred_element_type=jnp.float32
            ).astype(jnp.bfloat16)
            out_buf[r * n_virt + i, hh, :, :, cols] = update.reshape(A_UNIT, sb_here, tile_r)
            return carry

        lax.fori_loop(0, nrows // tile_r, tile, 0)
        out_copy(r, i, hh).start()

    def tables():
        sort_out[...] = unit_matrix(1, A_UNIT, sb_here)
        for i in range(nv // 128):
            piece = jnp.broadcast_to(row_ref[0:1, i * 128 : (i + 1) * 128], (128, 128))
            levels[i * 128 : (i + 1) * 128, :] = piece.T
        index = pair_ref[...]

        def add_level(o, acc):
            return acc + jnp.where(index == o, eocc_ref[o], 0.0)

        picked = lax.fori_loop(0, nocc, add_level, jnp.zeros(index.shape, jnp.float32))
        slot = lax.broadcasted_iota(jnp.int32, (1, nrows), 1)
        for hh in range(irreps_here):
            occ[hh : hh + 1, :] = picked[hh, 0:1, :] + picked[hh, 1:2, :]
            live = slot < pcount_ref[me_p * irreps_here + hh]
            occ[irreps_here + hh : irreps_here + hh + 1, :] = jnp.where(live, 1.0, 0.0)
        pick[0] = unit_matrix(1, slabs, a_rows)
        pick[1] = unit_matrix(1, 1, tile_m)
        terms[...] = jnp.zeros_like(terms)

    x_copy(0, 0).start()
    a_copy(0).start()
    barrier = pltpu.get_barrier_semaphore()
    for d in range(1, n_pair):
        pl.semaphore_signal(barrier, inc=1, device_id=(me_v, flip_bits(me_p, d, n_pair)), device_id_type=MESH)
    for d in range(1, n_virt):
        pl.semaphore_signal(barrier, inc=1, device_id=(flip_bits(me_v, d, n_virt), me_p), device_id_type=MESH)
    sort_in[...] = unit_matrix(1, irreps, A_UNIT)
    tables()
    pl.semaphore_wait(barrier, n_pair - 1 + n_virt - 1)

    prepare(0, 0, first=True)

    def one_round(r, carry):
        for i in range(n_virt):
            for hh in range(irreps_here):
                if i == 0:

                    @pl.when(r == 0)
                    def _():
                        load_amps(hh)
                        fetch_first(hh)

                    if hh == 0:

                        @pl.when(r > 0)
                        def _():
                            fetch(r, i)

                elif hh == 0:
                    fetch(r, i)
                compute(r, i, hh)
                if i == 0:

                    @pl.when(r == 0)
                    def _():
                        if hh + 1 < irreps_here:
                            prepare(0, hh + 1)
                        else:
                            for k in range(hh + 1, depth):
                                prepare(0, k)

            for d in range(1, n_pair):
                pair_copy(r, i, d).wait_send()
            if i + depth < n_virt:
                prepare(r, i + depth)
            else:

                @pl.when(r + 1 < rounds)
                def _():
                    prepare(r + 1, i + depth - n_virt)

        return carry

    lax.fori_loop(0, rounds, one_round, 0)
    for d in range(1, n_virt):
        part_copy(d).start()
    for d in range(1, n_virt):
        part_copy(d).wait()
    mine = terms[:, pl.ds(pl.multiple_of(me_v * e_cols, e_cols), e_cols)]
    for d in range(1, n_virt):
        mine = mine + parts[d - 1]
    energy_ref[...] = mine / energy_scale

    def drain(r, carry):
        for i in range(n_virt):
            for hh in range(irreps_here):
                out_copy(r, i, hh).wait()
        return carry

    lax.fori_loop(0, rounds, drain, 0)


def turn_kernel(in_ref, energy_ref, out_ref, energy_out, turned, sem):
    irreps_here, units, unit, n_virt, sb_here, rows = in_ref.shape
    slots, block = turned.shape[:2]
    per_a = n_virt * sb_here
    group = block // per_a
    per = rows // block
    eye = unit_matrix(1, 1, block)

    def out_copy(i):
        at = pl.multiple_of((i % per) * block, block)
        return pltpu.make_async_copy(turned.at[i % slots], out_ref.at[i // per, pl.ds(at, block)], sem.at[i % slots])

    def step(i, carry):
        @pl.when(i >= slots)
        def _():
            out_copy(i - slots).wait()

        cols = pl.ds(pl.multiple_of((i % per) * block, block), block)
        for u in range(units):
            for a in range(0, unit, group):
                piece = in_ref[i // per, u, a : a + group, :, :, cols].reshape(block, block)
                lanes = (u * unit + a) * per_a
                if (a // group) % 2:
                    turned[i % slots, :, lanes : lanes + block] = piece.T
                else:
                    turned[i % slots, :, lanes : lanes + block] = lax.dot_general(
                        eye, piece, (((1,), (1,)), ((), ())), preferred_element_type=jnp.float32
                    ).astype(jnp.bfloat16)
        out_copy(i).start()
        return carry

    count = irreps_here * per
    energy_out[...] = energy_ref[...]
    lax.fori_loop(0, count, step, 0)
    for i in range(max(count - slots, 0), count):
        out_copy(i).wait()


def fused_shards(amplitudes, integrals, virt_counts, pair_counts, pair_list, eps_occ, eps_virt):
    irreps_here, rows, slabs, ks = amplitudes.shape
    n_virt = lax.axis_size("virt")
    n_pair = lax.axis_size("pair")
    nv = integrals.shape[1]
    irreps = integrals.shape[2]
    loc = integrals.shape[3]
    depth = 4
    a_local = nv // n_virt
    units = a_local // A_UNIT
    steps = n_virt * units
    parts_sb = loc // ks
    sb_here = n_pair * parts_sb
    a_rows = 256 // slabs

    eri = integrals.reshape(slabs, nv * irreps, loc)
    pairs = jnp.transpose(pair_list, (0, 2, 1))
    vmem = pl.BlockSpec(memory_space=pltpu.VMEM)
    smem = pl.BlockSpec(memory_space=pltpu.SMEM)
    hbm = pl.BlockSpec(memory_space=pl.ANY)
    got, _, energy = pl.pallas_call(
        functools.partial(ladder_kernel, n_virt, n_pair, irreps_here, depth, parts_sb, nv * BLK),
        out_shape=(
            pltpu.VMEM((irreps_here, units, A_UNIT, n_virt, sb_here, rows), jnp.bfloat16),
            jax.ShapeDtypeStruct((units * n_virt, n_pair, irreps_here, slabs, A_UNIT, loc), jnp.bfloat16),
            pltpu.VMEM((irreps_here, rows // n_virt), jnp.float32),
        ),
        in_specs=[hbm, hbm, vmem, vmem, smem, smem, smem, smem],
        out_specs=(vmem, hbm, vmem),
        scratch_shapes=[
            pltpu.VMEM((slabs, A_UNIT * irreps, loc), jnp.bfloat16),
            pltpu.VMEM((depth, n_pair, irreps_here, slabs, A_UNIT, loc), jnp.bfloat16),
            pltpu.VMEM((n_pair, irreps_here, slabs, A_UNIT, loc), jnp.bfloat16),
            pltpu.VMEM((units * n_virt, irreps_here, A_UNIT, sb_here, rows), jnp.bfloat16),
            pltpu.VMEM((2, a_rows, slabs, ks), jnp.bfloat16),
            pltpu.VMEM((irreps_here, slabs, ks, rows), jnp.bfloat16),
            pltpu.VMEM((A_UNIT * irreps, A_UNIT * irreps), jnp.bfloat16),
            pltpu.VMEM((A_UNIT * sb_here, A_UNIT * sb_here), jnp.bfloat16),
            pltpu.VMEM((2, 256, 256), jnp.bfloat16),
            pltpu.VMEM((nv, 128), jnp.float32),
            pltpu.VMEM((2 * irreps_here, rows), jnp.float32),
            pltpu.VMEM((2, A_UNIT * sb_here, 1), jnp.float32),
            pltpu.VMEM((irreps_here, rows), jnp.float32),
            pltpu.VMEM((n_virt - 1, irreps_here, rows // n_virt), jnp.float32),
            pltpu.SemaphoreType.DMA,
            pltpu.SemaphoreType.DMA,
            pltpu.SemaphoreType.DMA((depth,)),
            pltpu.SemaphoreType.DMA((units, irreps_here)),
            pltpu.SemaphoreType.DMA((depth, n_pair - 1)),
            pltpu.SemaphoreType.DMA((steps, n_pair - 1)),
            pltpu.SemaphoreType.DMA((steps, irreps_here)),
            pltpu.SemaphoreType.DMA((steps, irreps_here)),
            pltpu.SemaphoreType.DMA((n_virt - 1,)),
            pltpu.SemaphoreType.DMA((n_virt - 1,)),
            pltpu.SemaphoreType.DMA((2,)),
            pltpu.SemaphoreType.DMA((irreps_here, n_pair - 1)),
        ],
        compiler_params=pltpu.CompilerParams(
            collective_id=0, has_side_effects=True, vmem_limit_bytes=44 * 1024 * 1024
        ),
    )(eri, amplitudes, pairs, eps_virt.reshape(1, nv), virt_counts, pair_counts, eps_occ, eps_virt)
    update, energy = pl.pallas_call(
        turn_kernel,
        out_shape=(
            jax.ShapeDtypeStruct((irreps_here, rows, a_local * BLK), jnp.bfloat16),
            jax.ShapeDtypeStruct((irreps_here, rows // n_virt), jnp.float32),
        ),
        in_specs=[vmem, vmem],
        out_specs=(hbm, vmem),
        scratch_shapes=[
            pltpu.VMEM((3, 256, a_local * BLK), jnp.bfloat16),
            pltpu.SemaphoreType.DMA((3,)),
        ],
        compiler_params=pltpu.CompilerParams(vmem_limit_bytes=12 * 1024 * 1024),
    )(
        pltpu.with_memory_space_constraint(got, pltpu.VMEM),
        pltpu.with_memory_space_constraint(energy, pltpu.VMEM),
    )
    return (update, energy)


def solution(mesh):
    placed = (
        P("pair", None, None, None),
        P(None, None, None, ("virt", "pair")),
        P(),
        P(),
        P("pair", None, None),
        P(),
        P(),
    )

    def run(*arrays):
        amplitudes, integrals = arrays[:2]
        loc = integrals.shape[3] // (mesh.shape["virt"] * mesh.shape["pair"])
        whole_slots = loc % amplitudes.shape[3] == 0
        whole_chunks = (integrals.shape[1] // mesh.shape["virt"]) % A_UNIT == 0
        body = fused_shards if whole_slots and whole_chunks else shards
        return jax.shard_map(
            body,
            mesh=mesh,
            in_specs=placed,
            out_specs=(P("pair", None, "virt"), P("pair", "virt")),
            check_vma=False,
        )(*arrays)

    return run
```

```python
import functools

import jax
import jax.numpy as jnp
from jax import lax
from jax.experimental import pallas as pl
from jax.experimental.pallas import tpu as pltpu
from jax.sharding import PartitionSpec as P

IRREPS = 8
NV = 512
BLK = 64
CS = 16
SLABS = 2
A_UNIT = 16
MESH = pl.DeviceIdType.MESH
TURNS = {8: (7, 6, 5, 4, 2, 3, 1, 0)}


def pick_counts(irrep_ids, table):
    onehot = irrep_ids[..., None] == jnp.arange(table.shape[0], dtype=jnp.int32)
    return jnp.sum(jnp.where(onehot, table, 0), axis=-1)


def shards(amplitudes, integrals, virt_counts, pair_counts, pair_list, eps_occ, eps_virt):
    local_irreps = amplitudes.shape[0]
    rows = amplitudes.shape[1]
    width = amplitudes.shape[3]
    n_virt = lax.axis_size("virt")
    n_pair = lax.axis_size("pair")
    a_local = NV // n_virt
    irrep_ids = lax.axis_index("pair") * local_irreps + jnp.arange(local_irreps, dtype=jnp.int32)
    slots = jnp.arange(BLK, dtype=jnp.int32)
    live_d = slots[None, :] < pick_counts(irrep_ids, virt_counts)[:, None]
    dmask = jnp.tile(live_d, (1, CS)).astype(jnp.bfloat16)
    masked = amplitudes * dmask[:, None, None, :]
    ladder = jnp.zeros((local_irreps, rows, a_local, BLK), jnp.float32)
    for s in range(SLABS):
        piece = integrals[s]
        moved = lax.all_to_all(
            lax.all_to_all(piece, "virt", split_axis=0, concat_axis=2, tiled=True),
            "pair",
            split_axis=1,
            concat_axis=2,
            tiled=True,
        )
        moved = moved.reshape(a_local, local_irreps, n_pair, n_virt, -1)
        moved = jnp.transpose(moved, (0, 1, 3, 2, 4)).reshape(a_local, local_irreps, BLK, width)
        ladder = ladder + jnp.einsum(
            "hrk,ahsk->hras", masked[:, :, s, :], moved, preferred_element_type=jnp.float32
        )
    a_global = lax.axis_index("virt") * a_local + jnp.arange(a_local, dtype=jnp.int32)
    a_irrep = a_global // BLK
    a_slot = a_global % BLK
    live_a = a_slot < pick_counts(a_irrep, virt_counts)
    eps_a = lax.dynamic_slice_in_dim(eps_virt, lax.axis_index("virt") * a_local, a_local)
    b_irrep = jnp.bitwise_xor(a_irrep[None, :], irrep_ids[:, None])
    b_onehot = (b_irrep[..., None] == jnp.arange(IRREPS, dtype=jnp.int32)).astype(jnp.float32)
    eps_table = eps_virt.reshape(IRREPS, BLK)
    eps_b = jnp.einsum("hag,gs->has", b_onehot, eps_table, precision=lax.Precision.HIGHEST)
    live_b = slots[None, None, :] < pick_counts(b_irrep, virt_counts)[..., None]
    occ_onehot = pair_list[..., None] == jnp.arange(eps_occ.shape[0], dtype=jnp.int32)
    occ_terms = jnp.sum(jnp.where(occ_onehot, eps_occ, 0.0), axis=-1)
    occ = occ_terms[:, :, 0] + occ_terms[:, :, 1]
    live_rows = (
        jnp.arange(rows, dtype=jnp.int32)[None, :] < pick_counts(irrep_ids, pair_counts)[:, None]
    )
    denom = (eps_a[None, :, None] + eps_b)[:, None, :, :] - occ[:, :, None, None]
    live = live_rows[:, :, None, None] & live_a[None, None, :, None] & live_b[:, None, :, :]
    ratio = jnp.where(live, ladder / denom, jnp.zeros_like(ladder))
    update = ratio.astype(jnp.bfloat16).reshape(local_irreps, rows, a_local * BLK)
    partial_value = jnp.sum(ratio * ladder, axis=(2, 3)) / (NV * BLK)
    energy = lax.psum_scatter(partial_value, "virt", scatter_dimension=1, tiled=True)
    return (update, energy)


def flip_bits(index, pattern, count):
    flipped = 0
    weight = 1
    while weight < count:
        bit = (index // weight) % 2
        mine = (pattern // weight) % 2
        flipped = flipped + weight * (bit + mine - 2 * bit * mine)
        weight *= 2
    return flipped


def turn_order(count):
    return TURNS.get(count, tuple(range(count - 1, -1, -1)))


def unit_matrix(count, outer, inner):
    rows = lax.broadcasted_iota(jnp.int32, (count * outer * inner, count * outer * inner), 0)
    cols = lax.broadcasted_iota(jnp.int32, (count * outer * inner, count * outer * inner), 1)
    unit = rows // (outer * inner)
    within = rows % (outer * inner)
    source = unit * (outer * inner) + (within % inner) * outer + within // inner
    return (source == cols).astype(jnp.float32).astype(jnp.bfloat16)


def ladder_kernel(
    n_virt, n_pair, irreps_here, depth, parts_sb, energy_scale,
    eri_ref, amps_ref, pair_ref, row_ref, vcount_ref, pcount_ref, eocc_ref, evirt_ref,
    got_ref, recv_ref, energy_ref,
    x_buf, stage, y_buf, out_buf, a_buf, amps, sort_in, sort_out, pick, levels, occ, cols_buf, terms, parts,
    x_sem, y_sem, own_sem, keep_sem, send_sem, recv_sem, out_sem, got_sem, term_sem, part_sem, a_sem, first_sem,
):
    me_v = lax.axis_index("virt")
    me_p = lax.axis_index("pair")
    slabs = eri_ref.shape[0]
    loc = eri_ref.shape[2]
    irreps = irreps_here * n_pair
    ks = amps.shape[2]
    nrows = amps.shape[3]
    nv = row_ref.shape[1]
    nocc = eocc_ref.shape[0]
    a_local = nv // n_virt
    unit_rows = A_UNIT * irreps
    sb_here = n_pair * parts_sb
    out_rows = A_UNIT * sb_here
    order = turn_order(n_virt)
    rounds = a_local // A_UNIT
    e_cols = nrows // n_virt
    tile_n = 512
    tile_m = 256
    tile_r = 512
    a_rows = a_buf.shape[1]
    peers = [d for d in range(2, n_pair)] + [1]

    def target(i):
        return flip_bits(me_v, order[i], n_virt)

    def x_copy(r, i):
        at = pl.multiple_of((target(i) * rounds + r) * unit_rows, unit_rows)
        return pltpu.make_async_copy(eri_ref.at[:, pl.ds(at, unit_rows), :], x_buf, x_sem)

    def a_copy(block):
        per = nrows // a_rows
        at = pl.multiple_of((block % per) * a_rows, a_rows)
        return pltpu.make_async_copy(
            amps_ref.at[block // per, pl.ds(at, a_rows)], a_buf.at[block % 2], a_sem.at[block % 2]
        )

    def pair_copy(r, i, d):
        peer = flip_bits(me_p, d, n_pair)
        return pltpu.make_async_remote_copy(
            src_ref=stage.at[i % depth, peer],
            dst_ref=recv_ref.at[r * n_virt + i, me_p],
            send_sem=send_sem.at[i % depth, d - 1],
            recv_sem=recv_sem.at[r * n_virt + i, d - 1],
            device_id=(me_v, peer),
            device_id_type=MESH,
        )

    def first_copy(hh, d):
        peer = flip_bits(me_p, d, n_pair)
        return pltpu.make_async_remote_copy(
            src_ref=stage.at[0, peer, hh],
            dst_ref=recv_ref.at[0, me_p, hh],
            send_sem=send_sem.at[0, d - 1],
            recv_sem=first_sem.at[hh, d - 1],
            device_id=(me_v, peer),
            device_id_type=MESH,
        )

    def own_copy(r, i):
        return pltpu.make_async_copy(
            stage.at[i % depth, me_p], recv_ref.at[r * n_virt + i, me_p], own_sem.at[i % depth]
        )

    def out_copy(r, i, hh):
        here = out_buf.at[r * n_virt + i, hh]
        there = got_ref.at[hh, r, :, me_v]
        if order[i] == 0:
            return pltpu.make_async_copy(here, there, keep_sem.at[r, hh])
        return pltpu.make_async_remote_copy(
            src_ref=here,
            dst_ref=there,
            send_sem=out_sem.at[r * n_virt + i, hh],
            recv_sem=got_sem.at[r * n_virt + i, hh],
            device_id=(target(i), me_p),
            device_id_type=MESH,
        )

    def part_copy(d):
        dest = flip_bits(me_v, d, n_virt)
        cols = pl.ds(pl.multiple_of(dest * e_cols, e_cols), e_cols)
        return pltpu.make_async_remote_copy(
            src_ref=terms.at[:, cols],
            dst_ref=parts.at[d - 1],
            send_sem=term_sem.at[d - 1],
            recv_sem=part_sem.at[d - 1],
            device_id=(dest, me_p),
            device_id_type=MESH,
        )

    def prepare(r, i, first=False):
        x_copy(r, i).wait()

        def sort_tile(k, carry):
            cols = pl.ds(pl.multiple_of(k * tile_n, tile_n), tile_n)
            for s in range(slabs):
                sorted_rows = jnp.dot(
                    sort_in[...], x_buf[s, :, cols], preferred_element_type=jnp.float32
                ).astype(jnp.bfloat16)
                for h in range(irreps):
                    stage[i % depth, h // irreps_here, h % irreps_here, s, :, cols] = sorted_rows[
                        h * A_UNIT : (h + 1) * A_UNIT
                    ]
            return carry

        lax.fori_loop(0, loc // tile_n, sort_tile, 0)
        if i + 1 < n_virt:
            x_copy(r, i + 1).start()
        else:

            @pl.when(r + 1 < rounds)
            def _():
                x_copy(r + 1, 0).start()

        if first:
            for hh in range(irreps_here):
                for d in peers:
                    first_copy(hh, d).start()
        else:
            for d in peers:
                pair_copy(r, i, d).start()
        own_copy(r, i).start()

    def load_amps(hh):
        per = nrows // a_rows
        h = me_p * irreps_here + hh
        slot = lax.broadcasted_iota(jnp.int32, (1, tile_m), 1) % BLK
        dmask = jnp.where(slot < vcount_ref[h], 1.0, 0.0).astype(jnp.bfloat16)

        def block(i, carry):
            now = hh * per + i
            a_copy(now).wait()

            @pl.when(now + 1 < irreps_here * per)
            def _():
                a_copy(now + 1).start()

            rows = pl.ds(pl.multiple_of(i * a_rows, a_rows), a_rows)
            for c in range(ks // tile_m):
                lanes = slice(c * tile_m, (c + 1) * tile_m)
                mixed = a_buf[now % 2, :, :, lanes].reshape(a_rows * slabs, tile_m)
                split = jnp.dot(pick[0], mixed, preferred_element_type=jnp.float32).astype(jnp.bfloat16) * dmask
                turned = lax.dot_general(
                    pick[1], split, (((1,), (1,)), ((), ())), preferred_element_type=jnp.float32
                ).astype(jnp.bfloat16)
                for s in range(slabs):
                    amps[hh, s, lanes, rows] = turned[:, s * a_rows : (s + 1) * a_rows]
            return carry

        lax.fori_loop(0, per, block, 0)

    def fetch(r, i):
        for d in range(1, n_pair):
            pair_copy(r, i, d).wait_recv()
        own_copy(r, i).wait()
        load = pltpu.make_async_copy(recv_ref.at[r * n_virt + i], y_buf, y_sem)
        load.start()
        load.wait()

    def fetch_first(hh):
        for d in range(1, n_pair):
            first_copy(hh, d).wait_recv()
        if hh == 0:
            own_copy(0, 0).wait()
        load = pltpu.make_async_copy(recv_ref.at[0, :, hh], y_buf.at[:, hh], y_sem)
        load.start()
        load.wait()

    def compute(r, i, hh):
        h = me_p * irreps_here + hh
        a_first = target(i) * a_local + r * A_UNIT
        a_irrep = a_first // BLK
        b_irrep = flip_bits(a_irrep, h, irreps)
        eps_a = levels[pl.ds(pl.multiple_of(a_first, A_UNIT), A_UNIT), 0:1]
        a_slot = a_first % BLK + lax.broadcasted_iota(jnp.int32, (A_UNIT, 1), 0)
        live_a = jnp.where(a_slot < vcount_ref[a_irrep], 1.0, 0.0)
        bases = []
        lives = []
        for b in range(sb_here):
            b_slot = me_v * sb_here + b
            bases.append(eps_a + evirt_ref[b_irrep * BLK + b_slot])
            lives.append(live_a * jnp.where(b_slot < vcount_ref[b_irrep], 1.0, 0.0))
        cols_buf[0] = jnp.concatenate(bases, axis=0)
        cols_buf[1] = jnp.concatenate(lives, axis=0)

        def tile(k, carry):
            cols = pl.ds(pl.multiple_of(k * tile_r, tile_r), tile_r)
            ladder = None
            for s in range(slabs):
                left = jnp.concatenate(
                    [y_buf[p, hh, s, :, j * ks : (j + 1) * ks] for p in range(n_pair) for j in range(parts_sb)],
                    axis=0,
                )
                term = jnp.dot(left, amps[hh, s, :, cols], preferred_element_type=jnp.float32)
                ladder = term if ladder is None else ladder + term
            denom = cols_buf[0] - occ[hh : hh + 1, cols]
            live = cols_buf[1] * occ[irreps_here + hh : irreps_here + hh + 1, cols]
            ratio = jnp.where(live > 0.5, ladder / denom, 0.0)
            terms[hh : hh + 1, cols] += jnp.sum(ratio * ladder, axis=0, keepdims=True)
            update = jnp.dot(
                sort_out[...], ratio.astype(jnp.bfloat16), preferred_element_type=jnp.float32
            ).astype(jnp.bfloat16)
            out_buf[r * n_virt + i, hh, :, :, cols] = update.reshape(A_UNIT, sb_here, tile_r)
            return carry

        lax.fori_loop(0, nrows // tile_r, tile, 0)
        out_copy(r, i, hh).start()

    def tables():
        sort_out[...] = unit_matrix(1, A_UNIT, sb_here)
        for i in range(nv // 128):
            piece = jnp.broadcast_to(row_ref[0:1, i * 128 : (i + 1) * 128], (128, 128))
            levels[i * 128 : (i + 1) * 128, :] = piece.T
        index = pair_ref[...]

        def add_level(o, acc):
            return acc + jnp.where(index == o, eocc_ref[o], 0.0)

        picked = lax.fori_loop(0, nocc, add_level, jnp.zeros(index.shape, jnp.float32))
        slot = lax.broadcasted_iota(jnp.int32, (1, nrows), 1)
        for hh in range(irreps_here):
            occ[hh : hh + 1, :] = picked[hh, 0:1, :] + picked[hh, 1:2, :]
            live = slot < pcount_ref[me_p * irreps_here + hh]
            occ[irreps_here + hh : irreps_here + hh + 1, :] = jnp.where(live, 1.0, 0.0)
        pick[0] = unit_matrix(1, slabs, a_rows)
        pick[1] = unit_matrix(1, 1, tile_m)
        terms[...] = jnp.zeros_like(terms)

    x_copy(0, 0).start()
    a_copy(0).start()
    barrier = pltpu.get_barrier_semaphore()
    for d in range(1, n_pair):
        pl.semaphore_signal(barrier, inc=1, device_id=(me_v, flip_bits(me_p, d, n_pair)), device_id_type=MESH)
    for d in range(1, n_virt):
        pl.semaphore_signal(barrier, inc=1, device_id=(flip_bits(me_v, d, n_virt), me_p), device_id_type=MESH)
    sort_in[...] = unit_matrix(1, irreps, A_UNIT)
    tables()
    pl.semaphore_wait(barrier, n_pair - 1 + n_virt - 1)

    prepare(0, 0, first=True)

    def one_round(r, carry):
        for i in range(n_virt):
            for hh in range(irreps_here):
                if i == 0:

                    @pl.when(r == 0)
                    def _():
                        load_amps(hh)
                        fetch_first(hh)

                    if hh == 0:

                        @pl.when(r > 0)
                        def _():
                            fetch(r, i)

                elif hh == 0:
                    fetch(r, i)
                compute(r, i, hh)
                if i == 0:

                    @pl.when(r == 0)
                    def _():
                        if hh + 1 < irreps_here:
                            prepare(0, hh + 1)
                        else:
                            for k in range(hh + 1, depth):
                                prepare(0, k)

            for d in range(1, n_pair):
                pair_copy(r, i, d).wait_send()
            if i + depth < n_virt:
                prepare(r, i + depth)
            else:

                @pl.when(r + 1 < rounds)
                def _():
                    prepare(r + 1, i + depth - n_virt)

        return carry

    lax.fori_loop(0, rounds, one_round, 0)
    for d in range(1, n_virt):
        part_copy(d).start()
    for d in range(1, n_virt):
        part_copy(d).wait()
    mine = terms[:, pl.ds(pl.multiple_of(me_v * e_cols, e_cols), e_cols)]
    for d in range(1, n_virt):
        mine = mine + parts[d - 1]
    energy_ref[...] = mine / energy_scale

    def drain(r, carry):
        for i in range(n_virt):
            for hh in range(irreps_here):
                out_copy(r, i, hh).wait()
        return carry

    lax.fori_loop(0, rounds, drain, 0)


def turn_kernel(in_ref, energy_ref, out_ref, energy_out, turned, sem):
    irreps_here, units, unit, n_virt, sb_here, rows = in_ref.shape
    slots, block = turned.shape[:2]
    per_a = n_virt * sb_here
    group = block // per_a
    per = rows // block
    eye = unit_matrix(1, 1, block)

    width = unit * per_a

    def out_copy(i, u):
        at = pl.multiple_of((i % per) * block, block)
        lanes = slice(u * width, (u + 1) * width)
        return pltpu.make_async_copy(
            turned.at[i % slots, :, lanes], out_ref.at[i // per, pl.ds(at, block), lanes], sem.at[i % slots, u]
        )

    def step(i, carry):
        @pl.when(i >= slots)
        def _():
            for u in range(units):
                out_copy(i - slots, u).wait()

        cols = pl.ds(pl.multiple_of((i % per) * block, block), block)
        for u in range(units):
            for a in range(0, unit, group):
                piece = in_ref[i // per, u, a : a + group, :, :, cols].reshape(block, block)
                lanes = (u * unit + a) * per_a
                if (a // group) % 2:
                    turned[i % slots, :, lanes : lanes + block] = piece.T
                else:
                    turned[i % slots, :, lanes : lanes + block] = lax.dot_general(
                        eye, piece, (((1,), (1,)), ((), ())), preferred_element_type=jnp.float32
                    ).astype(jnp.bfloat16)
            out_copy(i, u).start()
        return carry

    count = irreps_here * per
    energy_out[...] = energy_ref[...]
    lax.fori_loop(0, count, step, 0)
    for i in range(max(count - slots, 0), count):
        for u in range(units):
            out_copy(i, u).wait()


def fused_shards(amplitudes, integrals, virt_counts, pair_counts, pair_list, eps_occ, eps_virt):
    irreps_here, rows, slabs, ks = amplitudes.shape
    n_virt = lax.axis_size("virt")
    n_pair = lax.axis_size("pair")
    nv = integrals.shape[1]
    irreps = integrals.shape[2]
    loc = integrals.shape[3]
    depth = 4
    a_local = nv // n_virt
    units = a_local // A_UNIT
    steps = n_virt * units
    parts_sb = loc // ks
    sb_here = n_pair * parts_sb
    a_rows = 256 // slabs

    eri = integrals.reshape(slabs, nv * irreps, loc)
    pairs = jnp.transpose(pair_list, (0, 2, 1))
    vmem = pl.BlockSpec(memory_space=pltpu.VMEM)
    smem = pl.BlockSpec(memory_space=pltpu.SMEM)
    hbm = pl.BlockSpec(memory_space=pl.ANY)
    got, _, energy = pl.pallas_call(
        functools.partial(ladder_kernel, n_virt, n_pair, irreps_here, depth, parts_sb, nv * BLK),
        out_shape=(
            pltpu.VMEM((irreps_here, units, A_UNIT, n_virt, sb_here, rows), jnp.bfloat16),
            jax.ShapeDtypeStruct((units * n_virt, n_pair, irreps_here, slabs, A_UNIT, loc), jnp.bfloat16),
            pltpu.VMEM((irreps_here, rows // n_virt), jnp.float32),
        ),
        in_specs=[hbm, hbm, vmem, vmem, smem, smem, smem, smem],
        out_specs=(vmem, hbm, vmem),
        scratch_shapes=[
            pltpu.VMEM((slabs, A_UNIT * irreps, loc), jnp.bfloat16),
            pltpu.VMEM((depth, n_pair, irreps_here, slabs, A_UNIT, loc), jnp.bfloat16),
            pltpu.VMEM((n_pair, irreps_here, slabs, A_UNIT, loc), jnp.bfloat16),
            pltpu.VMEM((units * n_virt, irreps_here, A_UNIT, sb_here, rows), jnp.bfloat16),
            pltpu.VMEM((2, a_rows, slabs, ks), jnp.bfloat16),
            pltpu.VMEM((irreps_here, slabs, ks, rows), jnp.bfloat16),
            pltpu.VMEM((A_UNIT * irreps, A_UNIT * irreps), jnp.bfloat16),
            pltpu.VMEM((A_UNIT * sb_here, A_UNIT * sb_here), jnp.bfloat16),
            pltpu.VMEM((2, 256, 256), jnp.bfloat16),
            pltpu.VMEM((nv, 128), jnp.float32),
            pltpu.VMEM((2 * irreps_here, rows), jnp.float32),
            pltpu.VMEM((2, A_UNIT * sb_here, 1), jnp.float32),
            pltpu.VMEM((irreps_here, rows), jnp.float32),
            pltpu.VMEM((n_virt - 1, irreps_here, rows // n_virt), jnp.float32),
            pltpu.SemaphoreType.DMA,
            pltpu.SemaphoreType.DMA,
            pltpu.SemaphoreType.DMA((depth,)),
            pltpu.SemaphoreType.DMA((units, irreps_here)),
            pltpu.SemaphoreType.DMA((depth, n_pair - 1)),
            pltpu.SemaphoreType.DMA((steps, n_pair - 1)),
            pltpu.SemaphoreType.DMA((steps, irreps_here)),
            pltpu.SemaphoreType.DMA((steps, irreps_here)),
            pltpu.SemaphoreType.DMA((n_virt - 1,)),
            pltpu.SemaphoreType.DMA((n_virt - 1,)),
            pltpu.SemaphoreType.DMA((2,)),
            pltpu.SemaphoreType.DMA((irreps_here, n_pair - 1)),
        ],
        compiler_params=pltpu.CompilerParams(
            collective_id=0, has_side_effects=True, vmem_limit_bytes=44 * 1024 * 1024
        ),
    )(eri, amplitudes, pairs, eps_virt.reshape(1, nv), virt_counts, pair_counts, eps_occ, eps_virt)
    update, energy = pl.pallas_call(
        turn_kernel,
        out_shape=(
            jax.ShapeDtypeStruct((irreps_here, rows, a_local * BLK), jnp.bfloat16),
            jax.ShapeDtypeStruct((irreps_here, rows // n_virt), jnp.float32),
        ),
        in_specs=[vmem, vmem],
        out_specs=(hbm, vmem),
        scratch_shapes=[
            pltpu.VMEM((3, 256, a_local * BLK), jnp.bfloat16),
            pltpu.SemaphoreType.DMA((3, units)),
        ],
        compiler_params=pltpu.CompilerParams(vmem_limit_bytes=12 * 1024 * 1024),
    )(
        pltpu.with_memory_space_constraint(got, pltpu.VMEM),
        pltpu.with_memory_space_constraint(energy, pltpu.VMEM),
    )
    return (update, energy)


def solution(mesh):
    placed = (
        P("pair", None, None, None),
        P(None, None, None, ("virt", "pair")),
        P(),
        P(),
        P("pair", None, None),
        P(),
        P(),
    )

    def run(*arrays):
        amplitudes, integrals = arrays[:2]
        loc = integrals.shape[3] // (mesh.shape["virt"] * mesh.shape["pair"])
        whole_slots = loc % amplitudes.shape[3] == 0
        whole_chunks = (integrals.shape[1] // mesh.shape["virt"]) % A_UNIT == 0
        body = fused_shards if whole_slots and whole_chunks else shards
        return jax.shard_map(
            body,
            mesh=mesh,
            in_specs=placed,
            out_specs=(P("pair", None, "virt"), P("pair", "virt")),
            check_vma=False,
        )(*arrays)

    return run
```
